32 devices in a mesh: group: 2 (over y), ctx: 4 (over x, core), tp: 4 (over z).
Axes of the slice: x: 2, y: 2, z: 4, core: 2. Of those that a mesh axis runs over, the one named last changes fastest.
Arguments:
- tokens: bfloat16 [1024, 5376], P(('group', 'ctx'), 'tp'), parts along dimension 0
- positions: int32 [1024], P(('group', 'ctx')), parts along dimension 0, may hold values from 0 to 383, as said below
- first_key: int32 [1024], P(('group', 'ctx')), parts along dimension 0, may hold values from 0 to 511, as said below
- input_gain: float32 [5376], replicated, may hold values from 0.1 to 1.9
- query_weight: bfloat16 [5376, 4096], P(None, 'tp'), may hold values from -0.078125 to 0.078125
- kv_weight: bfloat16 [2, 5376, 2048], P(None, None, 'tp'), may hold values from -0.078125 to 0.078125
- query_gain: float32 [128], replicated, may hold values from 0.1 to 1.9
- key_gain: float32 [128], replicated, may hold values from 0.1 to 1.9
- out_weight: bfloat16 [4096, 5376], P('tp'), may hold values from -0.125 to 0.125
- post_gain: float32 [5376], replicated, may hold values from 0.1 to 1.9
Outputs:
- layer_out: bfloat16 [1024, 5376], P(('group', 'ctx'), 'tp'), parts along dimension 0
The draws below stay inside these ranges and needn't reach their ends.
There are 2 independent parts, one for each index of `group`. The reference program is written for one: setup_inputs(seed, part) draws one part's arguments, and reference() takes and returns one part's arrays. A program takes and returns all parts, laid end to end along the dimension named above; an argument that names none is the same for every part. Nothing has to cross between parts.
Inputs may be any that keep to these rules, and one draw needn't show every extreme that they name: `positions`: A token's position is its offset within its document. Documents are contiguous runs of tokens; exactly one of them is 384 tokens long, every other one is shorter, and the last token forms a document of its own. first_key[i] is the larger of i - 1023 and the index of the first token of i's document (documents as described for positions).
All inputs are finite; a program needn't handle non-finite values.
Results may differ from the reference program's by a relative error of at most 0.014.
Values may be sent and summed in bfloat16 or wider, within the bound.
A program may use at most 128 MiB of HBM per device.

```python
import math
import jax
import jax.numpy as jnp
from jax import lax

D = 5376
H = 32
KVH = 16
HD = 128
WINDOW = 1024
SEQ = 512
N_TP = 4


def draw_tokens(key, part):
    base_key, row_key, col_key = jax.random.split(key, 3)
    col_place = jnp.arange(D, dtype=jnp.float32) / D
    col_jitter = jax.random.uniform(col_key, (D,), jnp.float32)
    row_level = jax.random.uniform(row_key, (SEQ, 1), jnp.float32)
    base = jax.random.normal(base_key, (SEQ, D), jnp.float32)
    col_level = 0.5 * col_place + 0.5 * col_jitter - 0.5
    values = base * jnp.power(10.0, row_level - 0.5) * jnp.power(10.0, col_level)[None, :]
    return values.astype(jnp.bfloat16)


def document_starts(key):
    offset_key, cut_key = jax.random.split(jax.random.fold_in(key, 11))
    quarter = SEQ // 4
    long_start = jax.random.randint(offset_key, (), 0, quarter)
    token_index = jnp.arange(SEQ, dtype=jnp.int32)
    cut_here = jax.random.randint(cut_key, (SEQ,), 0, 32) == 0
    inside = (token_index >= long_start) & (token_index < long_start + SEQ - quarter)
    begins = cut_here & jnp.logical_not(inside) | (token_index == long_start) | (token_index == long_start + SEQ - quarter) | (token_index == 0) | (token_index == SEQ - 1)
    marker = jnp.where(begins, token_index, 0).astype(jnp.int32)
    return (token_index, lax.cummax(marker))


def draw_positions(key, part):
    token_index, start_of = document_starts(key)
    return (token_index - start_of).astype(jnp.int32)


def draw_first_key(key, part):
    token_index, start_of = document_starts(key)
    return jnp.maximum(start_of, token_index - WINDOW + 1).astype(jnp.int32)


def with_spikes(drawn, stream_key, source, target, blocks, factor):
    owner, partner = [(jnp.arange(drawn.shape[position]) // (drawn.shape[position] // blocks)).reshape([-1 if axis == position else 1 for axis in range(drawn.ndim)]) for position in (source, target)]
    chosen = jax.random.permutation(stream_key, blocks)[partner]
    strong = (owner == chosen) | (owner == (partner + blocks // 2) % blocks)
    return jnp.where(strong, factor * drawn, drawn)


def block_levels(stream_key, dims, pieces, least, high):
    level = 1.0
    for position, blocks in pieces:
        steps = jax.random.uniform(jax.random.fold_in(jax.random.fold_in(stream_key, 6), position), (blocks,), jnp.float32, least / len(pieces), high / len(pieces))
        level = level * jnp.repeat(jnp.exp(steps), dims[position] // blocks).reshape((-1,) + (1,) * (len(dims) - 1 - position))
    return level


def normal_values(rng, shape, deviation, bound, pieces=(), kind=jnp.bfloat16):
    loudness = block_levels(rng, shape, pieces, -0.22, 0.18) if pieces else 1.0
    drawn = jax.random.normal(rng, shape, jnp.float32) * deviation * loudness
    return jnp.minimum(jnp.maximum(drawn, -bound), bound).astype(kind)


def bell_draw_with(rng, extent, width, most, cuts, heavy, kind=jnp.bfloat16):
    array = width * jax.random.normal(rng, extent, jnp.float32)
    if cuts:
        array = array * block_levels(rng, extent, cuts, -0.22, 0.18)
    return jnp.clip(with_spikes(array, jax.random.fold_in(rng, 3), *heavy), -most, most).astype(kind)


def setup_inputs(seed: int = 0, part: int = 0) -> dict:
    arg_keys = jax.random.split(jax.random.key(seed), 11)
    part_splits = jax.random.split(jax.random.fold_in(arg_keys[10], part), 11)
    return {
        "tokens": draw_tokens(jax.random.fold_in(jax.random.fold_in(arg_keys[10], part), 71), part),
        "positions": draw_positions(jax.random.fold_in(jax.random.fold_in(arg_keys[10], part), 71), part),
        "first_key": draw_first_key(jax.random.fold_in(jax.random.fold_in(arg_keys[10], part), 71), part),
        "input_gain": jnp.clip(1.0 + 0.18 * jax.random.normal(arg_keys[3], (D,), jnp.float32), 0.1, 1.9),
        "query_weight": normal_values(arg_keys[4], (D, H * HD), D ** -0.5, 0.078125, ((1, 4),)),
        "kv_weight": normal_values(arg_keys[5], (2, D, KVH * HD), D ** -0.5, 0.078125, ((2, 4),)),
        "query_gain": jnp.clip(1.0 + 0.18 * jax.random.normal(arg_keys[6], (HD,), jnp.float32), 0.1, 1.9),
        "key_gain": jnp.clip(1.0 + 0.18 * jax.random.normal(arg_keys[7], (HD,), jnp.float32), 0.1, 1.9),
        "out_weight": bell_draw_with(arg_keys[8], (H * HD, D), (H * HD) ** -0.5, 0.125, ((0, 4),), (0, 1, 4, 2.0)),
        "post_gain": jnp.clip(1.0 + 0.18 * jax.random.normal(arg_keys[9], (D,), jnp.float32), 0.1, 1.9),
    }


EPSILON = 1e-06

def rms_norm(values, gain_vec):
    return values * lax.rsqrt(lax.optimization_barrier(jnp.mean(values * values, axis=-1, keepdims=True)) + EPSILON) * gain_vec

def rotate(values, positions_in):
    half_dim = values.shape[-1] // 2
    frequency = jnp.exp(jnp.arange(half_dim, dtype=jnp.float32) * (-2.0 * math.log(10000.0) / values.shape[-1]))
    angles = positions_in.astype(jnp.float32)[:, None] * frequency[None, :]
    cosines = jnp.cos(angles)[:, None, :]
    sine_part = jnp.sin(angles)[:, None, :]
    lower_half = values[..., :half_dim]
    upper_half = values[..., half_dim:]
    return jnp.concatenate([lower_half * cosines - upper_half * sine_part, upper_half * cosines + lower_half * sine_part], axis=-1)

def reference(tokens, positions, first_key, input_gain, query_weight, kv_weight, query_gain, key_gain, out_weight, post_gain):
    seq_len = tokens.shape[0]
    token_x = tokens.astype(jnp.float32)
    normed = rms_norm(token_x, input_gain).astype(jnp.bfloat16)
    query_raw = jnp.dot(normed, query_weight, preferred_element_type=jnp.float32).reshape(seq_len, H, HD)
    key_raw = jnp.dot(normed, kv_weight[0], preferred_element_type=jnp.float32).reshape(seq_len, KVH, HD)
    value_raw = jnp.dot(normed, kv_weight[1], preferred_element_type=jnp.float32).reshape(seq_len, KVH, HD)
    queries = (rotate(rms_norm(query_raw, query_gain), positions) * (D // H) ** (-0.5)).astype(jnp.bfloat16)
    keys = rotate(rms_norm(key_raw, key_gain), positions).astype(jnp.bfloat16)
    values_b = value_raw.astype(jnp.bfloat16)
    token_index = jnp.arange(seq_len, dtype=jnp.int32)
    visible = (token_index[None, :] >= first_key[:, None]) & (token_index[None, :] <= token_index[:, None])

    def one_head(head):
        query_h = lax.dynamic_index_in_dim(queries, head, 1, keepdims=False)
        key_h = lax.dynamic_index_in_dim(keys, head // 2, 1, keepdims=False)
        value_h = lax.dynamic_index_in_dim(values_b, head // 2, 1, keepdims=False)
        scores = jnp.dot(query_h, key_h.T, preferred_element_type=jnp.float32)
        scores = jnp.where(visible, scores, -1e+30)
        row_max = lax.optimization_barrier(jnp.max(scores, axis=1, keepdims=True))
        weights = jnp.exp(scores - row_max)
        denominator = lax.optimization_barrier(jnp.sum(weights, axis=1, keepdims=True))
        mixed_out = jnp.dot(weights.astype(jnp.bfloat16), value_h, preferred_element_type=jnp.float32)
        return (mixed_out / denominator).astype(jnp.bfloat16)
    heads_out = lax.map(one_head, jnp.arange(H, dtype=jnp.int32))
    attn = jnp.transpose(heads_out, (1, 0, 2)).reshape(seq_len, H * HD)
    group_rows = H * HD // N_TP

    def add_group(running, group_id):
        attn_part = lax.dynamic_slice_in_dim(attn, group_id * group_rows, group_rows, 1)
        weight_part = lax.dynamic_slice_in_dim(out_weight, group_id * group_rows, group_rows, 0)
        partial_value = jnp.dot(attn_part, weight_part, preferred_element_type=jnp.float32).astype(jnp.bfloat16)
        partial_value = lax.optimization_barrier(partial_value)
        return (running + partial_value.astype(jnp.float32), None)
    summed, unused = lax.scan(add_group, jnp.zeros((seq_len, D), jnp.float32), jnp.arange(N_TP, dtype=jnp.int32))
    return (token_x + rms_norm(summed, post_gain)).astype(jnp.bfloat16)
```

```python
import math

import jax
import jax.numpy as jnp
from jax import lax
from jax.experimental import pallas as pl
from jax.experimental.pallas import tpu as pltpu
from jax.sharding import PartitionSpec as P

D = 5376
H = 32
WINDOW = 1024


EPSILON = 1e-06


def from_partner(array, axis, distance):
    return lax.ppermute(array, axis, [(i, i ^ 1 << distance) for i in range(lax.axis_size(axis))])


def passed_along(block, axis, distance):
    devices = range(lax.axis_size(axis))
    route = [(i - distance, i) for i in devices if i - distance in devices]
    return lax.ppermute(block, axis, route)


def rms_norm(values, gain_vec):
    return (
        values * lax.rsqrt(jnp.mean(values * values, axis=-1, keepdims=True) + EPSILON) * gain_vec
    )


def rotate(values, positions_in):
    half_dim = values.shape[-1] // 2
    frequency = jnp.exp(
        jnp.arange(half_dim, dtype=jnp.float32) * (-2.0 * math.log(10000.0) / values.shape[-1])
    )
    angles = positions_in.astype(jnp.float32)[:, None] * frequency[None, :]
    cosines = jnp.cos(angles)[:, None, :]
    sine_part = jnp.sin(angles)[:, None, :]
    lower_half = values[..., :half_dim]
    upper_half = values[..., half_dim:]
    return jnp.concatenate(
        [
            lower_half * cosines - upper_half * sine_part,
            upper_half * cosines + lower_half * sine_part,
        ],
        axis=-1,
    )


def per_device(
    tokens,
    positions,
    first_key,
    input_gain,
    query_weight,
    kv_weight,
    query_gain,
    key_gain,
    out_weight,
    post_gain,
):
    tok_rows = tokens.shape[0]
    feat_dev = tokens.shape[1]
    head_dim = query_gain.shape[0]
    heads_dev = query_weight.shape[1] // head_dim
    tp_index = lax.axis_index("tp")
    ctx_index = lax.axis_index("ctx")
    ctx_count = lax.axis_size("ctx")
    local_x = tokens.astype(jnp.float32)
    kv_full = kv_weight
    if heads_dev == 1:
        partner = from_partner(kv_weight, "tp", 0)
        is_even = tp_index % 2 == 0
        kv_full = jnp.where(
            is_even,
            jnp.concatenate([kv_weight, partner], axis=2),
            jnp.concatenate([partner, kv_weight], axis=2),
        )
    gathered = lax.all_gather(tokens, "tp", axis=1, tiled=True).astype(jnp.float32)
    normed = rms_norm(gathered, input_gain).astype(jnp.bfloat16)
    query_raw = jnp.dot(normed, query_weight, preferred_element_type=jnp.float32)
    key_raw = jnp.dot(normed, kv_full[0], preferred_element_type=jnp.float32)
    value_raw = jnp.dot(normed, kv_full[1], preferred_element_type=jnp.float32)
    kv_heads = key_raw.shape[1] // head_dim
    group_size = heads_dev // kv_heads
    queries = (
        rotate(rms_norm(query_raw.reshape(tok_rows, heads_dev, head_dim), query_gain), positions)
        * (D // H) ** (-0.5)
    ).astype(jnp.bfloat16)
    keys = rotate(
        rms_norm(key_raw.reshape(tok_rows, kv_heads, head_dim), key_gain), positions
    ).astype(jnp.bfloat16)
    values_b = value_raw.reshape(tok_rows, kv_heads, head_dim).astype(jnp.bfloat16)
    kv_block = jnp.stack([keys, values_b])
    reach_blocks = min(ctx_count - 1, (WINDOW + tok_rows - 2) // tok_rows)
    received = []
    moving = kv_block
    for offset in range(reach_blocks):
        moving = passed_along(moving, "ctx", 1)
        received.append(moving)
    blocks = received[::-1] + [kv_block]
    keys_all = jnp.concatenate(blocks, axis=1)
    key_count = keys_all.shape[1]
    key_index = (ctx_index - reach_blocks) * tok_rows + jnp.arange(key_count, dtype=jnp.int32)
    query_index = ctx_index * tok_rows + jnp.arange(tok_rows, dtype=jnp.int32)
    visible = (key_index[None, :] >= first_key[:, None]) & (
        key_index[None, :] <= query_index[:, None]
    )
    grouped = queries.reshape(tok_rows, kv_heads, group_size, head_dim)
    scores = jnp.einsum("qkgd,tkd->kgqt", grouped, keys_all[0], preferred_element_type=jnp.float32)
    scores = jnp.where(visible[None, None], scores, -1e30)
    row_max = jnp.max(scores, axis=-1, keepdims=True)
    weights = jnp.exp(scores - row_max)
    denominator = jnp.sum(weights, axis=-1)
    mixed_out = jnp.einsum(
        "kgqt,tkd->qkgd",
        weights.astype(jnp.bfloat16),
        keys_all[1],
        preferred_element_type=jnp.float32,
    )
    mixed_out = mixed_out / jnp.transpose(denominator, (2, 0, 1))[..., None]
    attn = mixed_out.astype(jnp.bfloat16).reshape(tok_rows, heads_dev * head_dim)
    partial_value = jnp.dot(attn, out_weight, preferred_element_type=jnp.float32)
    summed = lax.psum(partial_value.astype(jnp.bfloat16), "tp").astype(jnp.float32)
    post_normed = rms_norm(summed, post_gain)
    own_cols = lax.dynamic_slice_in_dim(post_normed, tp_index * feat_dev, feat_dev, 1)
    return (local_x + own_cols).astype(jnp.bfloat16)


MESH = pl.DeviceIdType.MESH
F32 = jnp.float32
BF16 = jnp.bfloat16
TP = 4
CTX = 4
CHUNKS = 2
PRESCALE = 2.0**-10


def fused_kernel(
    tok_ref, pos_ref, fk_ref, ig_ref, qg_ref, kg_ref, pg_ref, qw_hbm, kvw_hbm, ow_hbm, out_ref,
    xbuf, xg_ref, wq, wkv, wo, gain_in, gain_post, ssq_ref, kv_acc, q_acc, cos_ref, sin_ref,
    kvbuf, q_ref, m_ref, l_ref, o_ref, attn_ref, part, rup, rdn, own, sq_mine, sq_all,
    w_sem, wo_sem, ag_up, ag_dn, ag_recv, kv_send, kv_recv,
    rs_up_send, rs_dn_send, rs_up_recv, rs_dn_recv, sq_send, sq_recv,
):
    rows, feat = tok_ref.shape
    hd = qg_ref.shape[1]
    kv_heads = wkv.shape[2] // hd
    heads = wq.shape[1] // hd
    model = feat * TP
    z = lax.axis_index("tp")
    c = lax.axis_index("ctx")
    partner = c + 1 - 2 * (c % 2)
    far = lax.rem(c + 2, CTX)
    crow = rows // CHUNKS
    ch_rows = [pl.ds(i * crow, crow) for i in range(CHUNKS)]

    def weight_copies(src):
        span = pl.ds(pl.multiple_of(src * feat, 64), feat)
        return (
            pltpu.make_async_copy(kvw_hbm.at[0, span], wkv.at[0, span], w_sem.at[src, 0]),
            pltpu.make_async_copy(kvw_hbm.at[1, span], wkv.at[1, span], w_sem.at[src, 1]),
            pltpu.make_async_copy(qw_hbm.at[span], wq.at[span], w_sem.at[src, 2]),
        )

    def each_source(fn):
        def at_distance(d, carry):
            @pl.when(z - d >= 0)
            def _():
                fn(z - d, d)

            @pl.when((z + d < TP) & (d > 0))
            def _():
                fn(z + d, d)

            return carry

        lax.fori_loop(0, TP, at_distance, 0)

    def begin_weights(src, d):
        for copy in weight_copies(src):
            copy.start()

    each_source(begin_weights)
    wo_copy = pltpu.make_async_copy(ow_hbm, wo, wo_sem)
    wo_copy.start()

    barrier = pltpu.get_barrier_semaphore()
    for d in range(1, TP):
        pl.semaphore_signal(
            barrier, inc=1, device_id={"tp": lax.rem(z + d, TP)}, device_id_type=MESH
        )
    pl.semaphore_signal(barrier, inc=1, device_id={"ctx": partner}, device_id_type=MESH)
    pl.semaphore_signal(barrier, inc=1, device_id={"ctx": far}, device_id_type=MESH)
    pl.semaphore_wait(barrier, TP + 1)

    up = {"tp": lax.rem(z + 1, TP)}
    down = {"tp": lax.rem(z + TP - 1, TP)}

    def ag_copy(source, src, ch, send, target):
        return pltpu.make_async_remote_copy(
            src_ref=source,
            dst_ref=xbuf.at[src, ch_rows[ch]],
            send_sem=send.at[src, ch],
            recv_sem=ag_recv.at[src, ch],
            device_id=target,
            device_id_type=MESH,
        )

    for ch in range(CHUNKS):
        @pl.when(z < TP - 1)
        def _():
            ag_copy(tok_ref.at[ch_rows[ch]], z, ch, ag_up, up).start()

        @pl.when(z > 0)
        def _():
            ag_copy(tok_ref.at[ch_rows[ch]], z, ch, ag_dn, down).start()

    for i in range(TP):
        gain_in[i] = ig_ref[:, i * feat : (i + 1) * feat] * PRESCALE
        gain_post[i] = pg_ref[:, i * feat : (i + 1) * feat]
    xbuf[z] = tok_ref[...]
    ssq_ref[...] = jnp.zeros_like(ssq_ref)
    kv_acc[...] = jnp.zeros_like(kv_acc)
    q_acc[...] = jnp.zeros_like(q_acc)
    r_iota = lax.broadcasted_iota(jnp.int32, (rows, rows), 0)
    c_iota = lax.broadcasted_iota(jnp.int32, (rows, rows), 1)
    diagonal = r_iota == c_iota

    def as_column(row):
        return jnp.sum(jnp.where(diagonal, row, 0.0), axis=1, keepdims=True)

    lane = lax.broadcasted_iota(jnp.int32, (rows, hd), 1)
    half = jnp.where(lane < hd // 2, lane, lane - hd // 2).astype(F32)
    angles = as_column(pos_ref[...].astype(F32)) * jnp.exp(half * (-2.0 * math.log(10000.0) / hd))
    cos_ref[...] = jnp.cos(angles)
    sines = jnp.sin(angles)
    sin_ref[...] = jnp.where(lane < hd // 2, -sines, sines)
    first = as_column(fk_ref[...].astype(F32)).astype(jnp.int32)

    last = jnp.where(z < TP // 2, TP - 1, 0)

    def query_product(src):
        span = pl.ds(pl.multiple_of(src * feat, 64), feat)
        weight_copies(src)[2].wait()
        q_acc[...] += jnp.dot(xg_ref[...], wq[span], preferred_element_type=F32)

    def projections(src):
        x = xbuf[src].astype(F32)
        ssq_ref[...] += jnp.sum(x * x, axis=1, keepdims=True)
        xg_ref[...] = (x * gain_in[src]).astype(BF16)
        span = pl.ds(pl.multiple_of(src * feat, 64), feat)
        width = wkv.shape[2]
        for i in range(2):
            weight_copies(src)[i].wait()
            kv_acc[:, i * width : (i + 1) * width] += jnp.dot(
                xg_ref[...], wkv[i, span], preferred_element_type=F32
            )

        @pl.when(src != last)
        def _():
            query_product(src)

    def at_distance(d, carry):
        low = z - d
        high = z + d
        for ch in range(CHUNKS):
            @pl.when((d > 0) & (low >= 0))
            def _():
                here = xbuf.at[low, ch_rows[ch]]
                ag_copy(here, low, ch, ag_up, down).wait_recv()

                @pl.when(z < TP - 1)
                def _():
                    ag_copy(here, low, ch, ag_up, up).start()

            @pl.when((d > 0) & (high < TP))
            def _():
                here = xbuf.at[high, ch_rows[ch]]
                ag_copy(here, high, ch, ag_dn, up).wait_recv()

                @pl.when(z > 0)
                def _():
                    ag_copy(here, high, ch, ag_dn, down).start()

        def side(i, inner):
            src = jnp.where(i == 0, low, high)

            @pl.when((src >= 0) & (src < TP) & ((d > 0) | (i == 0)))
            def _():
                projections(src)

            return inner

        lax.fori_loop(0, 2, side, 0)
        return carry

    lax.fori_loop(0, TP, at_distance, 0)

    inv = lax.rsqrt(ssq_ref[...] * (1.0 / model) + EPSILON) * (1.0 / PRESCALE)

    def normed_rotated(raw, gain_vec):
        raw = raw * inv
        scaled = raw * lax.rsqrt(jnp.mean(raw * raw, axis=1, keepdims=True) + EPSILON) * gain_vec
        return scaled * cos_ref[...] + pltpu.roll(scaled, hd // 2, 1) * sin_ref[...]

    width = kv_heads * hd
    for h in range(kv_heads):
        cols = slice(h * hd, (h + 1) * hd)
        kvbuf[c, 0, :, cols] = normed_rotated(kv_acc[:, cols], kg_ref[...]).astype(BF16)
    kvbuf[c, 1] = (kv_acc[:, width:] * inv).astype(BF16)

    def kv_copy(block, step, target):
        return pltpu.make_async_remote_copy(
            src_ref=kvbuf.at[block],
            dst_ref=kvbuf.at[block],
            send_sem=kv_send.at[step],
            recv_sem=kv_recv.at[step],
            device_id={"ctx": target},
            device_id_type=MESH,
        )

    @pl.when(c < CTX // 2)
    def _():
        kv_copy(c, 1, far).start()

    @pl.when(c % 2 == 0)
    def _():
        kv_copy(c, 0, partner).start()

    query_product(last)
    for h in range(heads):
        cols = slice(h * hd, (h + 1) * hd)
        spot = slice((h % 2) * rows, (h % 2 + 1) * rows)
        q_ref[h // 2, spot] = (
            normed_rotated(q_acc[:, cols], qg_ref[...]) * (D // H) ** (-0.5)
        ).astype(BF16)

    m_ref[...] = jnp.full_like(m_ref, -1e30)
    l_ref[...] = jnp.zeros_like(l_ref)
    o_ref[...] = jnp.zeros_like(o_ref)

    def attend(block):
        key_index = block * rows + c_iota
        visible = (key_index >= first) & (key_index <= c * rows + r_iota)
        bias = jnp.where(visible, 0.0, -1e30)
        bias = jnp.concatenate([bias, bias], axis=0)
        for h in range(kv_heads):
            cols = slice(h * hd, (h + 1) * hd)
            s = lax.dot_general(
                q_ref[h], kvbuf[block, 0, :, cols], (((1,), (1,)), ((), ())),
                preferred_element_type=F32,
            )
            s = jnp.where(bias < 0.0, -1e30, s)
            old = m_ref[h]
            new = jnp.maximum(old, jnp.max(s, axis=1, keepdims=True))
            fade = jnp.exp(old - new)
            p = jnp.exp(s - new)
            m_ref[h] = new
            l_ref[h] = l_ref[h] * fade + jnp.sum(p, axis=1, keepdims=True)
            o_ref[h] = o_ref[h] * fade + jnp.dot(
                p.astype(BF16), kvbuf[block, 1, :, cols], preferred_element_type=F32
            )

    def attention_step(step, carry):
        block = jnp.where(
            step == 0, c, jnp.where(step == 1, c - 1, jnp.where(step == 2, c - 2, partner - 2))
        )
        valid = (step == 0) | ((step == 1) & (c % 2 == 1)) | ((step >= 2) & (c >= CTX // 2))

        @pl.when(valid)
        def _():
            @pl.when(step > 0)
            def _():
                kv_copy(block, step - 1, partner).wait_recv()

            @pl.when(step == 2)
            def _():
                kv_copy(block, 2, partner).start()

            attend(block)

        return carry

    lax.fori_loop(0, CTX, attention_step, 0)

    for h in range(heads):
        spot = slice((h % 2) * rows, (h % 2 + 1) * rows)
        attn_ref[:, h * hd : (h + 1) * hd] = (
            o_ref[h // 2, spot] / l_ref[h // 2, spot]
        ).astype(BF16)

    wo_copy.wait()

    def rs_copy(dest, ch, buf, send, recv, target):
        return pltpu.make_async_remote_copy(
            src_ref=part.at[dest, ch_rows[ch]],
            dst_ref=buf.at[dest, ch_rows[ch]],
            send_sem=send.at[dest, ch],
            recv_sem=recv.at[dest, ch],
            device_id=target,
            device_id_type=MESH,
        )

    def rs_up(dest, ch):
        return rs_copy(dest, ch, rup, rs_up_send, rs_up_recv, up)

    def rs_dn(dest, ch):
        return rs_copy(dest, ch, rdn, rs_dn_send, rs_dn_recv, down)

    shift = feat % 128
    wide = feat + shift

    def out_step(k, carry):
        outer = TP - 1 - k
        inner = jnp.where(k == 0, 3, jnp.where(k == 1, 0, jnp.where(k == 2, 2, 1)))
        edge = (z == 0) | (z == TP - 1)
        dest = jnp.where(edge, outer, inner)
        dest = jnp.where(z < TP // 2, dest, TP - 1 - dest)
        odd = dest % 2
        start = pl.multiple_of((dest // 2) * (2 * feat) + odd * (feat - shift), 128)
        term = jnp.dot(
            attn_ref[...], wo[:, pl.ds(start, wide)], preferred_element_type=F32
        ).astype(BF16)

        @pl.when(odd == 0)
        def _():
            part[dest] = term[:, :feat]

        @pl.when(odd == 1)
        def _():
            part[dest] = term[:, shift:]

        for ch in range(CHUNKS):
            @pl.when((z == 0) & (dest > 0))
            def _():
                rs_up(dest, ch).start()

            @pl.when((z == TP - 1) & (dest < TP - 1))
            def _():
                rs_dn(dest, ch).start()

        return carry

    lax.fori_loop(0, TP, out_step, 0)
    own[...] = part[z].astype(F32)

    def sum_step(k, carry):
        for ch in range(CHUNKS):
            span = ch_rows[ch]
            for dest, has, onward, buf, copy in (
                (TP - 1 - k, (z > 0) & (TP - 1 - k >= z), TP - 1 - k > z, rup, rs_up),
                (k, (z < TP - 1) & (k <= z), k < z, rdn, rs_dn),
            ):
                @pl.when(has)
                def _():
                    copy(dest, ch).wait_recv()

                    @pl.when(onward)
                    def _():
                        part[dest, span] = (
                            part[dest, span].astype(F32) + buf[dest, span].astype(F32)
                        ).astype(BF16)
                        copy(dest, ch).start()

                    @pl.when(dest == z)
                    def _():
                        own[span] += buf[dest, span].astype(F32)

        return carry

    lax.fori_loop(0, TP, sum_step, 0)

    squares = jnp.sum(own[...] * own[...], axis=1, keepdims=True)
    as_row = jnp.sum(jnp.where(diagonal, squares, 0.0), axis=0, keepdims=True)
    sq_mine[...] = jnp.broadcast_to(as_row, sq_mine.shape)

    def sq_copy(d, slot):
        return pltpu.make_async_remote_copy(
            src_ref=sq_mine,
            dst_ref=sq_all.at[slot],
            send_sem=sq_send.at[d],
            recv_sem=sq_recv.at[slot],
            device_id={"tp": lax.rem(z + d, TP)},
            device_id_type=MESH,
        )

    for d in range(1, TP):
        sq_copy(d, z).start()
    for d in range(1, TP):
        slot = lax.rem(z + d, TP)
        sq_copy(d, slot).wait_recv()
        as_row = as_row + sq_all[slot, 0:1]
    inv_post = lax.rsqrt(as_column(as_row) * (1.0 / model) + EPSILON)
    out_ref[...] = (
        tok_ref[...].astype(F32) + own[...] * inv_post * gain_post[z]
    ).astype(BF16)

    for d in range(1, TP):
        sq_copy(d, z).wait_send()

    def settle(i, carry):
        for ch in range(CHUNKS):
            @pl.when((z < TP - 1) & (i <= z))
            def _():
                ag_copy(xbuf.at[i, ch_rows[ch]], i, ch, ag_up, up).wait_send()

            @pl.when((z > 0) & (i >= z))
            def _():
                ag_copy(xbuf.at[i, ch_rows[ch]], i, ch, ag_dn, down).wait_send()

            @pl.when(i > z)
            def _():
                rs_up(i, ch).wait_send()

            @pl.when(i < z)
            def _():
                rs_dn(i, ch).wait_send()

        return carry

    lax.fori_loop(0, TP, settle, 0)

    @pl.when(c < CTX // 2)
    def _():
        kv_copy(c, 1, far).wait_send()

    @pl.when(c % 2 == 0)
    def _():
        kv_copy(c, 0, partner).wait_send()

    @pl.when(c >= CTX // 2)
    def _():
        kv_copy(c - 2, 2, partner).wait_send()


def per_device_fused(
    tokens, positions, first_key, input_gain, query_weight, kv_weight, query_gain, key_gain,
    out_weight, post_gain,
):
    rows, feat = tokens.shape
    hd = query_gain.shape[0]
    q_cols = query_weight.shape[1]
    kv_cols = kv_weight.shape[2]
    model = query_weight.shape[0]
    kv_heads = kv_cols // hd
    vmem = pl.BlockSpec(memory_space=pltpu.VMEM)
    anywhere = pl.BlockSpec(memory_space=pl.ANY)
    dma = pltpu.SemaphoreType.DMA
    state = (kv_heads, 2 * rows, hd)
    return pl.pallas_call(
        fused_kernel,
        out_shape=jax.ShapeDtypeStruct((rows, feat), BF16),
        in_specs=[vmem] * 7 + [anywhere] * 3,
        out_specs=vmem,
        scratch_shapes=[
            pltpu.VMEM((TP, rows, feat), BF16),
            pltpu.VMEM((rows, feat), BF16),
            pltpu.VMEM((model, q_cols), BF16),
            pltpu.VMEM((2, model, kv_cols), BF16),
            pltpu.VMEM((q_cols, model), BF16),
            pltpu.VMEM((TP, 1, feat), F32),
            pltpu.VMEM((TP, 1, feat), F32),
            pltpu.VMEM((rows, 1), F32),
            pltpu.VMEM((rows, 2 * kv_cols), F32),
            pltpu.VMEM((rows, q_cols), F32),
            pltpu.VMEM((rows, hd), F32),
            pltpu.VMEM((rows, hd), F32),
            pltpu.VMEM((CTX, 2, rows, kv_cols), BF16),
            pltpu.VMEM(state, BF16),
            pltpu.VMEM((kv_heads, 2 * rows, 1), F32),
            pltpu.VMEM((kv_heads, 2 * rows, 1), F32),
            pltpu.VMEM(state, F32),
            pltpu.VMEM((rows, q_cols), BF16),
            pltpu.VMEM((TP, rows, feat), BF16),
            pltpu.VMEM((TP, rows, feat), BF16),
            pltpu.VMEM((TP, rows, feat), BF16),
            pltpu.VMEM((rows, feat), F32),
            pltpu.VMEM((8, rows), F32),
            pltpu.VMEM((TP, 8, rows), F32),
            dma((TP, 3)),
            dma,
            dma((TP, CHUNKS)),
            dma((TP, CHUNKS)),
            dma((TP, CHUNKS)),
            dma((3,)),
            dma((3,)),
            dma((TP, CHUNKS)),
            dma((TP, CHUNKS)),
            dma((TP, CHUNKS)),
            dma((TP, CHUNKS)),
            dma((TP,)),
            dma((TP,)),
        ],
        compiler_params=pltpu.CompilerParams(
            collective_id=0, has_side_effects=True, vmem_limit_bytes=60 * 1024 * 1024
        ),
    )(
        tokens,
        positions.reshape(1, rows),
        first_key.reshape(1, rows),
        input_gain.reshape(1, model),
        query_gain.reshape(1, hd),
        key_gain.reshape(1, hd),
        post_gain.reshape(1, model),
        query_weight,
        kv_weight,
        out_weight,
    )


def solution(mesh):
    fused = mesh.shape["tp"] == TP and mesh.shape["ctx"] == CTX
    return jax.shard_map(
        per_device_fused if fused else per_device,
        mesh=mesh,
        in_specs=(
            P(("group", "ctx"), "tp"),
            P(("group", "ctx")),
            P(("group", "ctx")),
            P(),
            P(None, "tp"),
            P(None, None, "tp"),
            P(),
            P(),
            P("tp", None),
            P(),
        ),
        out_specs=P(("group", "ctx"), "tp"),
        check_vma=False,
    )
```

```python
import math

import jax
import jax.numpy as jnp
from jax import lax
from jax.experimental import pallas as pl
from jax.experimental.pallas import tpu as pltpu
from jax.sharding import PartitionSpec as P

D = 5376
H = 32
WINDOW = 1024


EPSILON = 1e-06


def from_partner(array, axis, distance):
    return lax.ppermute(array, axis, [(i, i ^ 1 << distance) for i in range(lax.axis_size(axis))])


def passed_along(block, axis, distance):
    devices = range(lax.axis_size(axis))
    route = [(i - distance, i) for i in devices if i - distance in devices]
    return lax.ppermute(block, axis, route)


def rms_norm(values, gain_vec):
    return (
        values * lax.rsqrt(jnp.mean(values * values, axis=-1, keepdims=True) + EPSILON) * gain_vec
    )


def rotate(values, positions_in):
    half_dim = values.shape[-1] // 2
    frequency = jnp.exp(
        jnp.arange(half_dim, dtype=jnp.float32) * (-2.0 * math.log(10000.0) / values.shape[-1])
    )
    angles = positions_in.astype(jnp.float32)[:, None] * frequency[None, :]
    cosines = jnp.cos(angles)[:, None, :]
    sine_part = jnp.sin(angles)[:, None, :]
    lower_half = values[..., :half_dim]
    upper_half = values[..., half_dim:]
    return jnp.concatenate(
        [
            lower_half * cosines - upper_half * sine_part,
            upper_half * cosines + lower_half * sine_part,
        ],
        axis=-1,
    )


def per_device(
    tokens,
    positions,
    first_key,
    input_gain,
    query_weight,
    kv_weight,
    query_gain,
    key_gain,
    out_weight,
    post_gain,
):
    tok_rows = tokens.shape[0]
    feat_dev = tokens.shape[1]
    head_dim = query_gain.shape[0]
    heads_dev = query_weight.shape[1] // head_dim
    tp_index = lax.axis_index("tp")
    ctx_index = lax.axis_index("ctx")
    ctx_count = lax.axis_size("ctx")
    local_x = tokens.astype(jnp.float32)
    kv_full = kv_weight
    if heads_dev == 1:
        partner = from_partner(kv_weight, "tp", 0)
        is_even = tp_index % 2 == 0
        kv_full = jnp.where(
            is_even,
            jnp.concatenate([kv_weight, partner], axis=2),
            jnp.concatenate([partner, kv_weight], axis=2),
        )
    gathered = lax.all_gather(tokens, "tp", axis=1, tiled=True).astype(jnp.float32)
    normed = rms_norm(gathered, input_gain).astype(jnp.bfloat16)
    query_raw = jnp.dot(normed, query_weight, preferred_element_type=jnp.float32)
    key_raw = jnp.dot(normed, kv_full[0], preferred_element_type=jnp.float32)
    value_raw = jnp.dot(normed, kv_full[1], preferred_element_type=jnp.float32)
    kv_heads = key_raw.shape[1] // head_dim
    group_size = heads_dev // kv_heads
    queries = (
        rotate(rms_norm(query_raw.reshape(tok_rows, heads_dev, head_dim), query_gain), positions)
        * (D // H) ** (-0.5)
    ).astype(jnp.bfloat16)
    keys = rotate(
        rms_norm(key_raw.reshape(tok_rows, kv_heads, head_dim), key_gain), positions
    ).astype(jnp.bfloat16)
    values_b = value_raw.reshape(tok_rows, kv_heads, head_dim).astype(jnp.bfloat16)
    kv_block = jnp.stack([keys, values_b])
    reach_blocks = min(ctx_count - 1, (WINDOW + tok_rows - 2) // tok_rows)
    received = []
    moving = kv_block
    for offset in range(reach_blocks):
        moving = passed_along(moving, "ctx", 1)
        received.append(moving)
    blocks = received[::-1] + [kv_block]
    keys_all = jnp.concatenate(blocks, axis=1)
    key_count = keys_all.shape[1]
    key_index = (ctx_index - reach_blocks) * tok_rows + jnp.arange(key_count, dtype=jnp.int32)
    query_index = ctx_index * tok_rows + jnp.arange(tok_rows, dtype=jnp.int32)
    visible = (key_index[None, :] >= first_key[:, None]) & (
        key_index[None, :] <= query_index[:, None]
    )
    grouped = queries.reshape(tok_rows, kv_heads, group_size, head_dim)
    scores = jnp.einsum("qkgd,tkd->kgqt", grouped, keys_all[0], preferred_element_type=jnp.float32)
    scores = jnp.where(visible[None, None], scores, -1e30)
    row_max = jnp.max(scores, axis=-1, keepdims=True)
    weights = jnp.exp(scores - row_max)
    denominator = jnp.sum(weights, axis=-1)
    mixed_out = jnp.einsum(
        "kgqt,tkd->qkgd",
        weights.astype(jnp.bfloat16),
        keys_all[1],
        preferred_element_type=jnp.float32,
    )
    mixed_out = mixed_out / jnp.transpose(denominator, (2, 0, 1))[..., None]
    attn = mixed_out.astype(jnp.bfloat16).reshape(tok_rows, heads_dev * head_dim)
    partial_value = jnp.dot(attn, out_weight, preferred_element_type=jnp.float32)
    summed = lax.psum(partial_value.astype(jnp.bfloat16), "tp").astype(jnp.float32)
    post_normed = rms_norm(summed, post_gain)
    own_cols = lax.dynamic_slice_in_dim(post_normed, tp_index * feat_dev, feat_dev, 1)
    return (local_x + own_cols).astype(jnp.bfloat16)


MESH = pl.DeviceIdType.MESH
F32 = jnp.float32
BF16 = jnp.bfloat16
TP = 4
CTX = 4
CHUNKS = 2
PRESCALE = 2.0**-10


def fused_kernel(
    tok_ref, pos_ref, fk_ref, ig_ref, qg_ref, kg_ref, pg_ref, qw_hbm, kvw_hbm, ow_hbm, out_ref,
    xbuf, xg_ref, wq, wkv, wo, gain_in, gain_post, ssq_ref, kv_acc, q_acc, cos_ref, sin_ref,
    kvbuf, q_ref, m_ref, l_ref, o_ref, attn_ref, part, rup, rdn, own, sq_mine, sq_all,
    w_sem, wo_sem, ag_up, ag_dn, ag_recv, kv_send, kv_recv,
    rs_up_send, rs_dn_send, rs_up_recv, rs_dn_recv, sq_send, sq_recv,
):
    rows, feat = tok_ref.shape
    hd = qg_ref.shape[1]
    kv_heads = wkv.shape[2] // hd
    heads = wq.shape[1] // hd
    model = feat * TP
    z = lax.axis_index("tp")
    c = lax.axis_index("ctx")
    partner = c + 1 - 2 * (c % 2)
    far = lax.rem(c + 2, CTX)
    crow = rows // CHUNKS
    ch_rows = [pl.ds(i * crow, crow) for i in range(CHUNKS)]

    barrier = pltpu.get_barrier_semaphore()
    for d in range(1, TP):
        pl.semaphore_signal(
            barrier, inc=1, device_id={"tp": lax.rem(z + d, TP)}, device_id_type=MESH
        )
    pl.semaphore_signal(barrier, inc=1, device_id={"ctx": partner}, device_id_type=MESH)
    pl.semaphore_signal(barrier, inc=1, device_id={"ctx": far}, device_id_type=MESH)
    def weight_copies(src):
        span = pl.ds(pl.multiple_of(src * feat, 64), feat)
        return (
            pltpu.make_async_copy(kvw_hbm.at[0, span], wkv.at[0, span], w_sem.at[src, 0]),
            pltpu.make_async_copy(kvw_hbm.at[1, span], wkv.at[1, span], w_sem.at[src, 1]),
            pltpu.make_async_copy(qw_hbm.at[span], wq.at[span], w_sem.at[src, 2]),
        )

    def each_source(fn):
        def at_distance(d, carry):
            @pl.when(z - d >= 0)
            def _():
                fn(z - d, d)

            @pl.when((z + d < TP) & (d > 0))
            def _():
                fn(z + d, d)

            return carry

        lax.fori_loop(0, TP, at_distance, 0)

    def begin_weights(src, d):
        for copy in weight_copies(src):
            copy.start()

    each_source(begin_weights)
    wo_copy = pltpu.make_async_copy(ow_hbm, wo, wo_sem)
    wo_copy.start()

    pl.semaphore_wait(barrier, TP + 1)

    up = {"tp": lax.rem(z + 1, TP)}
    down = {"tp": lax.rem(z + TP - 1, TP)}

    def ag_copy(source, src, ch, send, target):
        return pltpu.make_async_remote_copy(
            src_ref=source,
            dst_ref=xbuf.at[src, ch_rows[ch]],
            send_sem=send.at[src, ch],
            recv_sem=ag_recv.at[src, ch],
            device_id=target,
            device_id_type=MESH,
        )

    for ch in range(CHUNKS):
        @pl.when(z < TP - 1)
        def _():
            ag_copy(tok_ref.at[ch_rows[ch]], z, ch, ag_up, up).start()

        @pl.when(z > 0)
        def _():
            ag_copy(tok_ref.at[ch_rows[ch]], z, ch, ag_dn, down).start()

    gains = ig_ref[...].reshape(1, model) * PRESCALE
    post_gains = pg_ref[...].reshape(1, model)
    for i in range(TP):
        gain_in[i] = gains[:, i * feat : (i + 1) * feat]
        gain_post[i] = post_gains[:, i * feat : (i + 1) * feat]
    xbuf[z] = tok_ref[...]
    ssq_ref[...] = jnp.zeros_like(ssq_ref)
    kv_acc[...] = jnp.zeros_like(kv_acc)
    q_acc[...] = jnp.zeros_like(q_acc)
    r_iota = lax.broadcasted_iota(jnp.int32, (rows, rows), 0)
    c_iota = lax.broadcasted_iota(jnp.int32, (rows, rows), 1)
    diagonal = r_iota == c_iota

    def as_column(row):
        return jnp.sum(jnp.where(diagonal, row, 0.0), axis=1, keepdims=True)

    lane = lax.broadcasted_iota(jnp.int32, (rows, hd), 1)
    half = jnp.where(lane < hd // 2, lane, lane - hd // 2).astype(F32)
    angles = as_column(pos_ref[...].astype(F32)) * jnp.exp(half * (-2.0 * math.log(10000.0) / hd))
    cos_ref[...] = jnp.cos(angles)
    sines = jnp.sin(angles)
    sin_ref[...] = jnp.where(lane < hd // 2, -sines, sines)
    first = as_column(fk_ref[...].astype(F32)).astype(jnp.int32)

    last = jnp.where(z < TP // 2, TP - 1, 0)

    def query_product(src):
        span = pl.ds(pl.multiple_of(src * feat, 64), feat)
        weight_copies(src)[2].wait()
        q_acc[...] += jnp.dot(xg_ref[...], wq[span], preferred_element_type=F32)

    def projections(src):
        x = xbuf[src].astype(F32)
        ssq_ref[...] += jnp.sum(x * x, axis=1, keepdims=True)
        xg_ref[...] = (x * gain_in[src]).astype(BF16)
        span = pl.ds(pl.multiple_of(src * feat, 64), feat)
        width = wkv.shape[2]
        for i in range(2):
            weight_copies(src)[i].wait()
            kv_acc[:, i * width : (i + 1) * width] += jnp.dot(
                xg_ref[...], wkv[i, span], preferred_element_type=F32
            )

        @pl.when(src != last)
        def _():
            query_product(src)

    def at_distance(d, carry):
        low = z - d
        high = z + d
        for ch in range(CHUNKS):
            @pl.when((d > 0) & (low >= 0))
            def _():
                here = xbuf.at[low, ch_rows[ch]]
                ag_copy(here, low, ch, ag_up, down).wait_recv()

                @pl.when(z < TP - 1)
                def _():
                    ag_copy(here, low, ch, ag_up, up).start()

            @pl.when((d > 0) & (high < TP))
            def _():
                here = xbuf.at[high, ch_rows[ch]]
                ag_copy(here, high, ch, ag_dn, up).wait_recv()

                @pl.when(z > 0)
                def _():
                    ag_copy(here, high, ch, ag_dn, down).start()

        def side(i, inner):
            src = jnp.where(i == 0, low, high)

            @pl.when((src >= 0) & (src < TP) & ((d > 0) | (i == 0)))
            def _():
                projections(src)

            return inner

        lax.fori_loop(0, 2, side, 0)
        return carry

    lax.fori_loop(0, TP, at_distance, 0)

    inv = lax.rsqrt(ssq_ref[...] * (1.0 / model) + EPSILON) * (1.0 / PRESCALE)

    def normed_rotated(raw, gain_vec):
        raw = raw * inv
        scaled = raw * lax.rsqrt(jnp.mean(raw * raw, axis=1, keepdims=True) + EPSILON) * gain_vec
        return scaled * cos_ref[...] + pltpu.roll(scaled, hd // 2, 1) * sin_ref[...]

    width = kv_heads * hd
    for h in range(kv_heads):
        cols = slice(h * hd, (h + 1) * hd)
        kvbuf[c, 0, :, cols] = normed_rotated(kv_acc[:, cols], kg_ref[...]).astype(BF16)
    kvbuf[c, 1] = (kv_acc[:, width:] * inv).astype(BF16)

    def kv_copy(block, step, target):
        return pltpu.make_async_remote_copy(
            src_ref=kvbuf.at[block],
            dst_ref=kvbuf.at[block],
            send_sem=kv_send.at[step],
            recv_sem=kv_recv.at[step],
            device_id={"ctx": target},
            device_id_type=MESH,
        )

    @pl.when(c < CTX // 2)
    def _():
        kv_copy(c, 1, far).start()

    @pl.when(c % 2 == 0)
    def _():
        kv_copy(c, 0, partner).start()

    query_product(last)
    for h in range(heads):
        cols = slice(h * hd, (h + 1) * hd)
        spot = slice((h % 2) * rows, (h % 2 + 1) * rows)
        q_ref[h // 2, spot] = (
            normed_rotated(q_acc[:, cols], qg_ref[...]) * (D // H) ** (-0.5)
        ).astype(BF16)

    m_ref[...] = jnp.full_like(m_ref, -1e30)
    l_ref[...] = jnp.zeros_like(l_ref)
    o_ref[...] = jnp.zeros_like(o_ref)

    def attend(block):
        key_index = block * rows + c_iota
        visible = (key_index >= first) & (key_index <= c * rows + r_iota)
        bias = jnp.where(visible, 0.0, -1e30)
        bias = jnp.concatenate([bias, bias], axis=0)
        for h in range(kv_heads):
            cols = slice(h * hd, (h + 1) * hd)
            s = lax.dot_general(
                q_ref[h], kvbuf[block, 0, :, cols], (((1,), (1,)), ((), ())),
                preferred_element_type=F32,
            )
            s = jnp.where(bias < 0.0, -1e30, s)
            old = m_ref[h]
            new = jnp.maximum(old, jnp.max(s, axis=1, keepdims=True))
            fade = jnp.exp(old - new)
            p = jnp.exp(s - new)
            m_ref[h] = new
            l_ref[h] = l_ref[h] * fade + jnp.sum(p, axis=1, keepdims=True)
            o_ref[h] = o_ref[h] * fade + jnp.dot(
                p.astype(BF16), kvbuf[block, 1, :, cols], preferred_element_type=F32
            )

    def attention_step(step, carry):
        block = jnp.where(
            step == 0, c, jnp.where(step == 1, c - 1, jnp.where(step == 2, c - 2, partner - 2))
        )
        valid = (step == 0) | ((step == 1) & (c % 2 == 1)) | ((step >= 2) & (c >= CTX // 2))

        @pl.when(valid)
        def _():
            @pl.when(step > 0)
            def _():
                kv_copy(block, step - 1, partner).wait_recv()

            @pl.when(step == 2)
            def _():
                kv_copy(block, 2, partner).start()

            attend(block)

        return carry

    lax.fori_loop(0, CTX, attention_step, 0)

    for h in range(heads):
        spot = slice((h % 2) * rows, (h % 2 + 1) * rows)
        attn_ref[:, h * hd : (h + 1) * hd] = (
            o_ref[h // 2, spot] / l_ref[h // 2, spot]
        ).astype(BF16)

    wo_copy.wait()

    def rs_copy(dest, ch, buf, send, recv, target):
        return pltpu.make_async_remote_copy(
            src_ref=part.at[dest, ch_rows[ch]],
            dst_ref=buf.at[dest, ch_rows[ch]],
            send_sem=send.at[dest, ch],
            recv_sem=recv.at[dest, ch],
            device_id=target,
            device_id_type=MESH,
        )

    def rs_up(dest, ch):
        return rs_copy(dest, ch, rup, rs_up_send, rs_up_recv, up)

    def rs_dn(dest, ch):
        return rs_copy(dest, ch, rdn, rs_dn_send, rs_dn_recv, down)

    shift = feat % 128
    wide = feat + shift

    def out_step(k, carry):
        outer = TP - 1 - k
        inner = jnp.where(k == 0, 3, jnp.where(k == 1, 0, jnp.where(k == 2, 2, 1)))
        edge = (z == 0) | (z == TP - 1)
        dest = jnp.where(edge, outer, inner)
        dest = jnp.where(z < TP // 2, dest, TP - 1 - dest)
        odd = dest % 2
        start = pl.multiple_of((dest // 2) * (2 * feat) + odd * (feat - shift), 128)
        term = jnp.dot(
            attn_ref[...], wo[:, pl.ds(start, wide)], preferred_element_type=F32
        ).astype(BF16)

        @pl.when(odd == 0)
        def _():
            part[dest] = term[:, :feat]

        @pl.when(odd == 1)
        def _():
            part[dest] = term[:, shift:]

        for ch in range(CHUNKS):
            @pl.when((z == 0) & (dest > 0))
            def _():
                rs_up(dest, ch).start()

            @pl.when((z == TP - 1) & (dest < TP - 1))
            def _():
                rs_dn(dest, ch).start()

        return carry

    lax.fori_loop(0, TP, out_step, 0)
    own[...] = part[z].astype(F32)

    def sum_step(k, carry):
        for ch in range(CHUNKS):
            span = ch_rows[ch]
            from_low = z + TP - 1 - k
            from_high = z + k - (TP - 1)
            for dest, has, buf, copy in (
                (from_low, (z > 0) & (from_low < TP), rup, rs_up),
                (from_high, (z < TP - 1) & (from_high >= 0), rdn, rs_dn),
            ):
                @pl.when(has)
                def _():
                    copy(dest, ch).wait_recv()

                    @pl.when(dest != z)
                    def _():
                        part[dest, span] = (
                            part[dest, span].astype(F32) + buf[dest, span].astype(F32)
                        ).astype(BF16)
                        copy(dest, ch).start()

                    @pl.when(dest == z)
                    def _():
                        own[span] += buf[dest, span].astype(F32)

        return carry

    lax.fori_loop(1, TP, sum_step, 0)

    squares = jnp.sum(own[...] * own[...], axis=1, keepdims=True)
    as_row = jnp.sum(jnp.where(diagonal, squares, 0.0), axis=0, keepdims=True)
    sq_mine[...] = jnp.broadcast_to(as_row, sq_mine.shape)

    def sq_copy(d, slot):
        return pltpu.make_async_remote_copy(
            src_ref=sq_mine,
            dst_ref=sq_all.at[slot],
            send_sem=sq_send.at[d],
            recv_sem=sq_recv.at[slot],
            device_id={"tp": lax.rem(z + d, TP)},
            device_id_type=MESH,
        )

    for d in range(1, TP):
        sq_copy(d, z).start()
    for d in range(1, TP):
        slot = lax.rem(z + d, TP)
        sq_copy(d, slot).wait_recv()
        as_row = as_row + sq_all[slot, 0:1]
    inv_post = lax.rsqrt(as_column(as_row) * (1.0 / model) + EPSILON)
    out_ref[...] = (
        tok_ref[...].astype(F32) + own[...] * inv_post * gain_post[z]
    ).astype(BF16)

    for d in range(1, TP):
        sq_copy(d, z).wait_send()

    def settle(i, carry):
        for ch in range(CHUNKS):
            @pl.when((z < TP - 1) & (i <= z))
            def _():
                ag_copy(xbuf.at[i, ch_rows[ch]], i, ch, ag_up, up).wait_send()

            @pl.when((z > 0) & (i >= z))
            def _():
                ag_copy(xbuf.at[i, ch_rows[ch]], i, ch, ag_dn, down).wait_send()

            @pl.when(i > z)
            def _():
                rs_up(i, ch).wait_send()

            @pl.when(i < z)
            def _():
                rs_dn(i, ch).wait_send()

        return carry

    lax.fori_loop(0, TP, settle, 0)

    @pl.when(c < CTX // 2)
    def _():
        kv_copy(c, 1, far).wait_send()

    @pl.when(c % 2 == 0)
    def _():
        kv_copy(c, 0, partner).wait_send()

    @pl.when(c >= CTX // 2)
    def _():
        kv_copy(c - 2, 2, partner).wait_send()


def per_device_fused(
    tokens, positions, first_key, input_gain, query_weight, kv_weight, query_gain, key_gain,
    out_weight, post_gain,
):
    rows, feat = tokens.shape
    hd = query_gain.shape[0]
    q_cols = query_weight.shape[1]
    kv_cols = kv_weight.shape[2]
    model = query_weight.shape[0]
    kv_heads = kv_cols // hd
    vmem = pl.BlockSpec(memory_space=pltpu.VMEM)
    anywhere = pl.BlockSpec(memory_space=pl.ANY)
    dma = pltpu.SemaphoreType.DMA
    state = (kv_heads, 2 * rows, hd)
    return pl.pallas_call(
        fused_kernel,
        out_shape=jax.ShapeDtypeStruct((rows, feat), BF16),
        in_specs=[vmem] * 7 + [anywhere] * 3,
        out_specs=vmem,
        scratch_shapes=[
            pltpu.VMEM((TP, rows, feat), BF16),
            pltpu.VMEM((rows, feat), BF16),
            pltpu.VMEM((model, q_cols), BF16),
            pltpu.VMEM((2, model, kv_cols), BF16),
            pltpu.VMEM((q_cols, model), BF16),
            pltpu.VMEM((TP, 1, feat), F32),
            pltpu.VMEM((TP, 1, feat), F32),
            pltpu.VMEM((rows, 1), F32),
            pltpu.VMEM((rows, 2 * kv_cols), F32),
            pltpu.VMEM((rows, q_cols), F32),
            pltpu.VMEM((rows, hd), F32),
            pltpu.VMEM((rows, hd), F32),
            pltpu.VMEM((CTX, 2, rows, kv_cols), BF16),
            pltpu.VMEM(state, BF16),
            pltpu.VMEM((kv_heads, 2 * rows, 1), F32),
            pltpu.VMEM((kv_heads, 2 * rows, 1), F32),
            pltpu.VMEM(state, F32),
            pltpu.VMEM((rows, q_cols), BF16),
            pltpu.VMEM((TP, rows, feat), BF16),
            pltpu.VMEM((TP, rows, feat), BF16),
            pltpu.VMEM((TP, rows, feat), BF16),
            pltpu.VMEM((rows, feat), F32),
            pltpu.VMEM((8, rows), F32),
            pltpu.VMEM((TP, 8, rows), F32),
            dma((TP, 3)),
            dma,
            dma((TP, CHUNKS)),
            dma((TP, CHUNKS)),
            dma((TP, CHUNKS)),
            dma((3,)),
            dma((3,)),
            dma((TP, CHUNKS)),
            dma((TP, CHUNKS)),
            dma((TP, CHUNKS)),
            dma((TP, CHUNKS)),
            dma((TP,)),
            dma((TP,)),
        ],
        compiler_params=pltpu.CompilerParams(
            collective_id=0, has_side_effects=True, vmem_limit_bytes=60 * 1024 * 1024
        ),
    )(
        tokens,
        positions.reshape(1, rows),
        first_key.reshape(1, rows),
        input_gain,
        query_gain.reshape(1, hd),
        key_gain.reshape(1, hd),
        post_gain,
        query_weight,
        kv_weight,
        out_weight,
    )


def solution(mesh):
    fused = mesh.shape["tp"] == TP and mesh.shape["ctx"] == CTX
    return jax.shard_map(
        per_device_fused if fused else per_device,
        mesh=mesh,
        in_specs=(
            P(("group", "ctx"), "tp"),
            P(("group", "ctx")),
            P(("group", "ctx")),
            P(),
            P(None, "tp"),
            P(None, None, "tp"),
            P(),
            P(),
            P("tp", None),
            P(),
        ),
        out_specs=P(("group", "ctx"), "tp"),
        check_vma=False,
    )
```

```python
import math

import jax
import jax.numpy as jnp
from jax import lax
from jax.experimental import pallas as pl
from jax.experimental.pallas import tpu as pltpu
from jax.sharding import PartitionSpec as P

D = 5376
H = 32
WINDOW = 1024


EPSILON = 1e-06


def from_partner(array, axis, distance):
    return lax.ppermute(array, axis, [(i, i ^ 1 << distance) for i in range(lax.axis_size(axis))])


def passed_along(block, axis, distance):
    devices = range(lax.axis_size(axis))
    route = [(i - distance, i) for i in devices if i - distance in devices]
    return lax.ppermute(block, axis, route)


def rms_norm(values, gain_vec):
    return (
        values * lax.rsqrt(jnp.mean(values * values, axis=-1, keepdims=True) + EPSILON) * gain_vec
    )


def rotate(values, positions_in):
    half_dim = values.shape[-1] // 2
    frequency = jnp.exp(
        jnp.arange(half_dim, dtype=jnp.float32) * (-2.0 * math.log(10000.0) / values.shape[-1])
    )
    angles = positions_in.astype(jnp.float32)[:, None] * frequency[None, :]
    cosines = jnp.cos(angles)[:, None, :]
    sine_part = jnp.sin(angles)[:, None, :]
    lower_half = values[..., :half_dim]
    upper_half = values[..., half_dim:]
    return jnp.concatenate(
        [
            lower_half * cosines - upper_half * sine_part,
            upper_half * cosines + lower_half * sine_part,
        ],
        axis=-1,
    )


def per_device(
    tokens,
    positions,
    first_key,
    input_gain,
    query_weight,
    kv_weight,
    query_gain,
    key_gain,
    out_weight,
    post_gain,
):
    tok_rows = tokens.shape[0]
    feat_dev = tokens.shape[1]
    head_dim = query_gain.shape[0]
    heads_dev = query_weight.shape[1] // head_dim
    tp_index = lax.axis_index("tp")
    ctx_index = lax.axis_index("ctx")
    ctx_count = lax.axis_size("ctx")
    local_x = tokens.astype(jnp.float32)
    kv_full = kv_weight
    if heads_dev == 1:
        partner = from_partner(kv_weight, "tp", 0)
        is_even = tp_index % 2 == 0
        kv_full = jnp.where(
            is_even,
            jnp.concatenate([kv_weight, partner], axis=2),
            jnp.concatenate([partner, kv_weight], axis=2),
        )
    gathered = lax.all_gather(tokens, "tp", axis=1, tiled=True).astype(jnp.float32)
    normed = rms_norm(gathered, input_gain).astype(jnp.bfloat16)
    query_raw = jnp.dot(normed, query_weight, preferred_element_type=jnp.float32)
    key_raw = jnp.dot(normed, kv_full[0], preferred_element_type=jnp.float32)
    value_raw = jnp.dot(normed, kv_full[1], preferred_element_type=jnp.float32)
    kv_heads = key_raw.shape[1] // head_dim
    group_size = heads_dev // kv_heads
    queries = (
        rotate(rms_norm(query_raw.reshape(tok_rows, heads_dev, head_dim), query_gain), positions)
        * (D // H) ** (-0.5)
    ).astype(jnp.bfloat16)
    keys = rotate(
        rms_norm(key_raw.reshape(tok_rows, kv_heads, head_dim), key_gain), positions
    ).astype(jnp.bfloat16)
    values_b = value_raw.reshape(tok_rows, kv_heads, head_dim).astype(jnp.bfloat16)
    kv_block = jnp.stack([keys, values_b])
    reach_blocks = min(ctx_count - 1, (WINDOW + tok_rows - 2) // tok_rows)
    received = []
    moving = kv_block
    for offset in range(reach_blocks):
        moving = passed_along(moving, "ctx", 1)
        received.append(moving)
    blocks = received[::-1] + [kv_block]
    keys_all = jnp.concatenate(blocks, axis=1)
    key_count = keys_all.shape[1]
    key_index = (ctx_index - reach_blocks) * tok_rows + jnp.arange(key_count, dtype=jnp.int32)
    query_index = ctx_index * tok_rows + jnp.arange(tok_rows, dtype=jnp.int32)
    visible = (key_index[None, :] >= first_key[:, None]) & (
        key_index[None, :] <= query_index[:, None]
    )
    grouped = queries.reshape(tok_rows, kv_heads, group_size, head_dim)
    scores = jnp.einsum("qkgd,tkd->kgqt", grouped, keys_all[0], preferred_element_type=jnp.float32)
    scores = jnp.where(visible[None, None], scores, -1e30)
    row_max = jnp.max(scores, axis=-1, keepdims=True)
    weights = jnp.exp(scores - row_max)
    denominator = jnp.sum(weights, axis=-1)
    mixed_out = jnp.einsum(
        "kgqt,tkd->qkgd",
        weights.astype(jnp.bfloat16),
        keys_all[1],
        preferred_element_type=jnp.float32,
    )
    mixed_out = mixed_out / jnp.transpose(denominator, (2, 0, 1))[..., None]
    attn = mixed_out.astype(jnp.bfloat16).reshape(tok_rows, heads_dev * head_dim)
    partial_value = jnp.dot(attn, out_weight, preferred_element_type=jnp.float32)
    summed = lax.psum(partial_value.astype(jnp.bfloat16), "tp").astype(jnp.float32)
    post_normed = rms_norm(summed, post_gain)
    own_cols = lax.dynamic_slice_in_dim(post_normed, tp_index * feat_dev, feat_dev, 1)
    return (local_x + own_cols).astype(jnp.bfloat16)


MESH = pl.DeviceIdType.MESH
F32 = jnp.float32
BF16 = jnp.bfloat16
TP = 4
CTX = 4
CHUNKS = 2
PRESCALE = 2.0**-10


def fused_kernel(
    tok_ref, pos_ref, fk_ref, ig_ref, qg_ref, kg_ref, pg_ref, qw_hbm, kvw_hbm, ow_hbm, out_ref,
    xbuf, xg_ref, tok_rows, wq, wkv, wo, gain_in, gain_post, ssq_ref, kv_acc, q_acc, cos_ref, sin_ref,
    kvbuf, q_ref, m_ref, l_ref, o_ref, attn_ref, part, rup, rdn, own, sq_mine, sq_all,
    w_sem, wo_sem, ag_up, ag_dn, ag_recv, kv_send, kv_recv,
    rs_up_send, rs_dn_send, rs_up_recv, rs_dn_recv, sq_send, sq_recv,
):
    feat, rows = tok_ref.shape
    piece = feat // CHUNKS
    hd = qg_ref.shape[1]
    kv_heads = wkv.shape[2] // hd
    heads = wq.shape[1] // hd
    model = feat * TP
    z = lax.axis_index("tp")
    c = lax.axis_index("ctx")
    partner = c + 1 - 2 * (c % 2)
    far = lax.rem(c + 2, CTX)
    crow = rows // CHUNKS
    ch_rows = [pl.ds(i * crow, crow) for i in range(CHUNKS)]

    barrier = pltpu.get_barrier_semaphore()
    for d in range(1, TP):
        pl.semaphore_signal(
            barrier, inc=1, device_id={"tp": lax.rem(z + d, TP)}, device_id_type=MESH
        )
    pl.semaphore_signal(barrier, inc=1, device_id={"ctx": partner}, device_id_type=MESH)
    pl.semaphore_signal(barrier, inc=1, device_id={"ctx": far}, device_id_type=MESH)
    def weight_span(src, ch):
        return pl.ds(pl.multiple_of(src * feat + ch * piece, 32), piece)

    def weight_copies(src, ch):
        span = weight_span(src, ch)
        return (
            pltpu.make_async_copy(kvw_hbm.at[0, span], wkv.at[0, span], w_sem.at[src, ch, 0]),
            pltpu.make_async_copy(kvw_hbm.at[1, span], wkv.at[1, span], w_sem.at[src, ch, 1]),
            pltpu.make_async_copy(qw_hbm.at[span], wq.at[span], w_sem.at[src, ch, 2]),
        )

    def each_source(fn):
        def at_distance(d, carry):
            @pl.when(z - d >= 0)
            def _():
                fn(z - d, d)

            @pl.when((z + d < TP) & (d > 0))
            def _():
                fn(z + d, d)

            return carry

        lax.fori_loop(0, TP, at_distance, 0)

    def begin_weights(src, d):
        for ch in range(CHUNKS):
            for copy in weight_copies(src, ch):
                copy.start()

    each_source(begin_weights)
    wo_copy = pltpu.make_async_copy(ow_hbm, wo, wo_sem)
    wo_copy.start()

    pl.semaphore_wait(barrier, TP + 1)

    up = {"tp": lax.rem(z + 1, TP)}
    down = {"tp": lax.rem(z + TP - 1, TP)}

    def piece_of(ch):
        return pl.ds(pl.multiple_of(ch * piece, 32), piece)

    def ag_copy(source, src, ch, send, target):
        return pltpu.make_async_remote_copy(
            src_ref=source,
            dst_ref=xbuf.at[src, piece_of(ch)],
            send_sem=send.at[src, ch],
            recv_sem=ag_recv.at[src, ch],
            device_id=target,
            device_id_type=MESH,
        )

    for ch in range(CHUNKS):
        @pl.when(z < TP - 1)
        def _():
            ag_copy(tok_ref.at[piece_of(ch)], z, ch, ag_up, up).start()

        @pl.when(z > 0)
        def _():
            ag_copy(tok_ref.at[piece_of(ch)], z, ch, ag_dn, down).start()

    gains = ig_ref[...].reshape(1, model) * PRESCALE
    post_gains = pg_ref[...].reshape(1, model)
    for i in range(TP * CHUNKS):
        gain_in[i] = gains[:, i * piece : (i + 1) * piece]
    for i in range(TP):
        gain_post[i] = post_gains[:, i * feat : (i + 1) * feat]
    xbuf[z] = tok_ref[...]
    ssq_ref[...] = jnp.zeros_like(ssq_ref)
    kv_acc[...] = jnp.zeros_like(kv_acc)
    q_acc[...] = jnp.zeros_like(q_acc)
    r_iota = lax.broadcasted_iota(jnp.int32, (rows, rows), 0)
    c_iota = lax.broadcasted_iota(jnp.int32, (rows, rows), 1)
    diagonal = r_iota == c_iota

    def as_column(row):
        return jnp.sum(jnp.where(diagonal, row, 0.0), axis=1, keepdims=True)

    lane = lax.broadcasted_iota(jnp.int32, (rows, hd), 1)
    half = jnp.where(lane < hd // 2, lane, lane - hd // 2).astype(F32)
    angles = as_column(pos_ref[...].astype(F32)) * jnp.exp(half * (-2.0 * math.log(10000.0) / hd))
    cos_ref[...] = jnp.cos(angles)
    sines = jnp.sin(angles)
    sin_ref[...] = jnp.where(lane < hd // 2, -sines, sines)
    first = as_column(fk_ref[...].astype(F32)).astype(jnp.int32)

    last = jnp.where(z < TP // 2, TP - 1, 0)

    def query_product(src, ch):
        weight_copies(src, ch)[2].wait()
        q_acc[...] += jnp.dot(
            xg_ref[...], wq[weight_span(src, ch)], preferred_element_type=F32
        )

    def projections(src, ch):
        x_t = xbuf[src, piece_of(ch)].astype(F32)
        ssq_ref[...] += jnp.sum(x_t * x_t, axis=0, keepdims=True)
        xg_ref[...] = (x_t.T * gain_in[src * CHUNKS + ch]).astype(BF16)
        width = wkv.shape[2]
        for i in range(2):
            weight_copies(src, ch)[i].wait()
            kv_acc[:, i * width : (i + 1) * width] += jnp.dot(
                xg_ref[...], wkv[i, weight_span(src, ch)], preferred_element_type=F32
            )

        @pl.when((src != last) | (ch < CHUNKS - 1))
        def _():
            query_product(src, ch)

    def gather_step(k, carry):
        d = k // CHUNKS
        ch = k % CHUNKS
        low = z - d
        high = z + d

        @pl.when((d > 0) & (low >= 0))
        def _():
            here = xbuf.at[low, piece_of(ch)]
            ag_copy(here, low, ch, ag_up, down).wait_recv()

            @pl.when(z < TP - 1)
            def _():
                ag_copy(here, low, ch, ag_up, up).start()

        @pl.when((d > 0) & (high < TP))
        def _():
            here = xbuf.at[high, piece_of(ch)]
            ag_copy(here, high, ch, ag_dn, up).wait_recv()

            @pl.when(z > 0)
            def _():
                ag_copy(here, high, ch, ag_dn, down).start()

        def side(i, inner):
            src = jnp.where(i == 0, low, high)

            @pl.when((src >= 0) & (src < TP) & ((d > 0) | (i == 0)))
            def _():
                projections(src, ch)

            return inner

        lax.fori_loop(0, 2, side, 0)
        return carry

    lax.fori_loop(0, TP * CHUNKS, gather_step, 0)

    inv = lax.rsqrt(as_column(ssq_ref[...]) * (1.0 / model) + EPSILON) * (1.0 / PRESCALE)

    def normed_rotated(raw, gain_vec):
        raw = raw * inv
        scaled = raw * lax.rsqrt(jnp.mean(raw * raw, axis=1, keepdims=True) + EPSILON) * gain_vec
        return scaled * cos_ref[...] + pltpu.roll(scaled, hd // 2, 1) * sin_ref[...]

    width = kv_heads * hd
    for h in range(kv_heads):
        cols = slice(h * hd, (h + 1) * hd)
        kvbuf[c, 0, :, cols] = normed_rotated(kv_acc[:, cols], kg_ref[...]).astype(BF16)
    kvbuf[c, 1] = (kv_acc[:, width:] * inv).astype(BF16)

    def kv_copy(block, step, target):
        return pltpu.make_async_remote_copy(
            src_ref=kvbuf.at[block],
            dst_ref=kvbuf.at[block],
            send_sem=kv_send.at[step],
            recv_sem=kv_recv.at[step],
            device_id={"ctx": target},
            device_id_type=MESH,
        )

    @pl.when(c < CTX // 2)
    def _():
        kv_copy(c, 1, far).start()

    @pl.when(c % 2 == 0)
    def _():
        kv_copy(c, 0, partner).start()

    query_product(last, CHUNKS - 1)
    for h in range(heads):
        cols = slice(h * hd, (h + 1) * hd)
        spot = slice((h % 2) * rows, (h % 2 + 1) * rows)
        q_ref[h // 2, spot] = (
            normed_rotated(q_acc[:, cols], qg_ref[...]) * (D // H) ** (-0.5)
        ).astype(BF16)

    m_ref[...] = jnp.full_like(m_ref, -1e30)
    l_ref[...] = jnp.zeros_like(l_ref)
    o_ref[...] = jnp.zeros_like(o_ref)

    def attend(block):
        key_index = block * rows + c_iota
        visible = (key_index >= first) & (key_index <= c * rows + r_iota)
        bias = jnp.where(visible, 0.0, -1e30)
        bias = jnp.concatenate([bias, bias], axis=0)
        for h in range(kv_heads):
            cols = slice(h * hd, (h + 1) * hd)
            s = lax.dot_general(
                q_ref[h], kvbuf[block, 0, :, cols], (((1,), (1,)), ((), ())),
                preferred_element_type=F32,
            )
            s = jnp.where(bias < 0.0, -1e30, s)
            old = m_ref[h]
            new = jnp.maximum(old, jnp.max(s, axis=1, keepdims=True))
            fade = jnp.exp(old - new)
            p = jnp.exp(s - new)
            m_ref[h] = new
            l_ref[h] = l_ref[h] * fade + jnp.sum(p, axis=1, keepdims=True)
            o_ref[h] = o_ref[h] * fade + jnp.dot(
                p.astype(BF16), kvbuf[block, 1, :, cols], preferred_element_type=F32
            )

    def attention_step(step, carry):
        block = jnp.where(
            step == 0, c, jnp.where(step == 1, c - 1, jnp.where(step == 2, c - 2, partner - 2))
        )
        valid = (step == 0) | ((step == 1) & (c % 2 == 1)) | ((step >= 2) & (c >= CTX // 2))

        @pl.when(valid)
        def _():
            @pl.when(step > 0)
            def _():
                kv_copy(block, step - 1, partner).wait_recv()

            @pl.when(step == 2)
            def _():
                kv_copy(block, 2, partner).start()

            attend(block)

        return carry

    lax.fori_loop(0, CTX, attention_step, 0)

    for h in range(heads):
        spot = slice((h % 2) * rows, (h % 2 + 1) * rows)
        attn_ref[:, h * hd : (h + 1) * hd] = (
            o_ref[h // 2, spot] / l_ref[h // 2, spot]
        ).astype(BF16)

    wo_copy.wait()

    def rs_copy(dest, ch, buf, send, recv, target):
        return pltpu.make_async_remote_copy(
            src_ref=part.at[dest, ch_rows[ch]],
            dst_ref=buf.at[dest, ch_rows[ch]],
            send_sem=send.at[dest, ch],
            recv_sem=recv.at[dest, ch],
            device_id=target,
            device_id_type=MESH,
        )

    def rs_up(dest, ch):
        return rs_copy(dest, ch, rup, rs_up_send, rs_up_recv, up)

    def rs_dn(dest, ch):
        return rs_copy(dest, ch, rdn, rs_dn_send, rs_dn_recv, down)

    shift = feat % 128
    wide = feat + shift

    def out_step(k, carry):
        outer = TP - 1 - k
        inner = jnp.where(k == 0, 3, jnp.where(k == 1, 0, jnp.where(k == 2, 2, 1)))
        edge = (z == 0) | (z == TP - 1)
        dest = jnp.where(edge, outer, inner)
        dest = jnp.where(z < TP // 2, dest, TP - 1 - dest)
        odd = dest % 2
        start = pl.multiple_of((dest // 2) * (2 * feat) + odd * (feat - shift), 128)
        term = jnp.dot(
            attn_ref[...], wo[:, pl.ds(start, wide)], preferred_element_type=F32
        ).astype(BF16)

        @pl.when(odd == 0)
        def _():
            part[dest] = term[:, :feat]

        @pl.when(odd == 1)
        def _():
            part[dest] = term[:, shift:]

        for ch in range(CHUNKS):
            @pl.when((z == 0) & (dest > 0))
            def _():
                rs_up(dest, ch).start()

            @pl.when((z == TP - 1) & (dest < TP - 1))
            def _():
                rs_dn(dest, ch).start()

        return carry

    lax.fori_loop(0, TP, out_step, 0)
    own[...] = part[z].astype(F32)
    tok_rows[...] = tok_ref[...].astype(F32).T

    def sum_step(k, carry):
        for ch in range(CHUNKS):
            span = ch_rows[ch]
            from_low = z + TP - 1 - k
            from_high = z + k - (TP - 1)
            for dest, has, buf, copy in (
                (from_low, (z > 0) & (from_low < TP), rup, rs_up),
                (from_high, (z < TP - 1) & (from_high >= 0), rdn, rs_dn),
            ):
                @pl.when(has)
                def _():
                    copy(dest, ch).wait_recv()

                    @pl.when(dest != z)
                    def _():
                        part[dest, span] = (
                            part[dest, span].astype(F32) + buf[dest, span].astype(F32)
                        ).astype(BF16)
                        copy(dest, ch).start()

                    @pl.when(dest == z)
                    def _():
                        own[span] += buf[dest, span].astype(F32)

        return carry

    lax.fori_loop(1, TP, sum_step, 0)

    squares = jnp.sum(own[...] * own[...], axis=1, keepdims=True)
    as_row = jnp.sum(jnp.where(diagonal, squares, 0.0), axis=0, keepdims=True)
    sq_mine[...] = jnp.broadcast_to(as_row, sq_mine.shape)

    def sq_copy(d, slot):
        return pltpu.make_async_remote_copy(
            src_ref=sq_mine,
            dst_ref=sq_all.at[slot],
            send_sem=sq_send.at[d],
            recv_sem=sq_recv.at[slot],
            device_id={"tp": lax.rem(z + d, TP)},
            device_id_type=MESH,
        )

    for d in range(1, TP):
        sq_copy(d, z).start()
    for d in range(1, TP):
        slot = lax.rem(z + d, TP)
        sq_copy(d, slot).wait_recv()
        as_row = as_row + sq_all[slot, 0:1]
    inv_post = lax.rsqrt(as_column(as_row) * (1.0 / model) + EPSILON)
    out_ref[...] = (
        tok_rows[...] + own[...] * inv_post * gain_post[z]
    ).astype(BF16)

    for d in range(1, TP):
        sq_copy(d, z).wait_send()

    def settle(i, carry):
        for ch in range(CHUNKS):
            @pl.when((z < TP - 1) & (i <= z))
            def _():
                ag_copy(xbuf.at[i, piece_of(ch)], i, ch, ag_up, up).wait_send()

            @pl.when((z > 0) & (i >= z))
            def _():
                ag_copy(xbuf.at[i, piece_of(ch)], i, ch, ag_dn, down).wait_send()

            @pl.when(i > z)
            def _():
                rs_up(i, ch).wait_send()

            @pl.when(i < z)
            def _():
                rs_dn(i, ch).wait_send()

        return carry

    lax.fori_loop(0, TP, settle, 0)

    @pl.when(c < CTX // 2)
    def _():
        kv_copy(c, 1, far).wait_send()

    @pl.when(c % 2 == 0)
    def _():
        kv_copy(c, 0, partner).wait_send()

    @pl.when(c >= CTX // 2)
    def _():
        kv_copy(c - 2, 2, partner).wait_send()


def per_device_fused(
    tokens, positions, first_key, input_gain, query_weight, kv_weight, query_gain, key_gain,
    out_weight, post_gain,
):
    feat, rows = tokens.shape[1], tokens.shape[0]
    piece = feat // CHUNKS
    hd = query_gain.shape[0]
    q_cols = query_weight.shape[1]
    kv_cols = kv_weight.shape[2]
    model = query_weight.shape[0]
    kv_heads = kv_cols // hd
    vmem = pl.BlockSpec(memory_space=pltpu.VMEM)
    anywhere = pl.BlockSpec(memory_space=pl.ANY)
    dma = pltpu.SemaphoreType.DMA
    state = (kv_heads, 2 * rows, hd)
    return pl.pallas_call(
        fused_kernel,
        out_shape=jax.ShapeDtypeStruct((rows, feat), BF16),
        in_specs=[vmem] * 7 + [anywhere] * 3,
        out_specs=vmem,
        scratch_shapes=[
            pltpu.VMEM((TP, feat, rows), BF16),
            pltpu.VMEM((rows, piece), BF16),
            pltpu.VMEM((rows, feat), F32),
            pltpu.VMEM((model, q_cols), BF16),
            pltpu.VMEM((2, model, kv_cols), BF16),
            pltpu.VMEM((q_cols, model), BF16),
            pltpu.VMEM((TP * CHUNKS, 1, piece), F32),
            pltpu.VMEM((TP, 1, feat), F32),
            pltpu.VMEM((1, rows), F32),
            pltpu.VMEM((rows, 2 * kv_cols), F32),
            pltpu.VMEM((rows, q_cols), F32),
            pltpu.VMEM((rows, hd), F32),
            pltpu.VMEM((rows, hd), F32),
            pltpu.VMEM((CTX, 2, rows, kv_cols), BF16),
            pltpu.VMEM(state, BF16),
            pltpu.VMEM((kv_heads, 2 * rows, 1), F32),
            pltpu.VMEM((kv_heads, 2 * rows, 1), F32),
            pltpu.VMEM(state, F32),
            pltpu.VMEM((rows, q_cols), BF16),
            pltpu.VMEM((TP, rows, feat), BF16),
            pltpu.VMEM((TP, rows, feat), BF16),
            pltpu.VMEM((TP, rows, feat), BF16),
            pltpu.VMEM((rows, feat), F32),
            pltpu.VMEM((8, rows), F32),
            pltpu.VMEM((TP, 8, rows), F32),
            dma((TP, CHUNKS, 3)),
            dma,
            dma((TP, CHUNKS)),
            dma((TP, CHUNKS)),
            dma((TP, CHUNKS)),
            dma((3,)),
            dma((3,)),
            dma((TP, CHUNKS)),
            dma((TP, CHUNKS)),
            dma((TP, CHUNKS)),
            dma((TP, CHUNKS)),
            dma((TP,)),
            dma((TP,)),
        ],
        compiler_params=pltpu.CompilerParams(
            collective_id=0, has_side_effects=True, vmem_limit_bytes=60 * 1024 * 1024
        ),
    )(
        tokens.T,
        positions.reshape(1, rows),
        first_key.reshape(1, rows),
        input_gain,
        query_gain.reshape(1, hd),
        key_gain.reshape(1, hd),
        post_gain,
        query_weight,
        kv_weight,
        out_weight,
    )


def solution(mesh):
    fused = mesh.shape["tp"] == TP and mesh.shape["ctx"] == CTX
    return jax.shard_map(
        per_device_fused if fused else per_device,
        mesh=mesh,
        in_specs=(
            P(("group", "ctx"), "tp"),
            P(("group", "ctx")),
            P(("group", "ctx")),
            P(),
            P(None, "tp"),
            P(None, None, "tp"),
            P(),
            P(),
            P("tp", None),
            P(),
        ),
        out_specs=P(("group", "ctx"), "tp"),
        check_vma=False,
    )
```

```python
import math

import jax
import jax.numpy as jnp
from jax import lax
from jax.experimental import pallas as pl
from jax.experimental.pallas import tpu as pltpu
from jax.sharding import PartitionSpec as P

D = 5376
H = 32
WINDOW = 1024


EPSILON = 1e-06


def from_partner(array, axis, distance):
    return lax.ppermute(array, axis, [(i, i ^ 1 << distance) for i in range(lax.axis_size(axis))])


def passed_along(block, axis, distance):
    devices = range(lax.axis_size(axis))
    route = [(i - distance, i) for i in devices if i - distance in devices]
    return lax.ppermute(block, axis, route)


def rms_norm(values, gain_vec):
    return (
        values * lax.rsqrt(jnp.mean(values * values, axis=-1, keepdims=True) + EPSILON) * gain_vec
    )


def rotate(values, positions_in):
    half_dim = values.shape[-1] // 2
    frequency = jnp.exp(
        jnp.arange(half_dim, dtype=jnp.float32) * (-2.0 * math.log(10000.0) / values.shape[-1])
    )
    angles = positions_in.astype(jnp.float32)[:, None] * frequency[None, :]
    cosines = jnp.cos(angles)[:, None, :]
    sine_part = jnp.sin(angles)[:, None, :]
    lower_half = values[..., :half_dim]
    upper_half = values[..., half_dim:]
    return jnp.concatenate(
        [
            lower_half * cosines - upper_half * sine_part,
            upper_half * cosines + lower_half * sine_part,
        ],
        axis=-1,
    )


def per_device(
    tokens,
    positions,
    first_key,
    input_gain,
    query_weight,
    kv_weight,
    query_gain,
    key_gain,
    out_weight,
    post_gain,
):
    tok_rows = tokens.shape[0]
    feat_dev = tokens.shape[1]
    head_dim = query_gain.shape[0]
    heads_dev = query_weight.shape[1] // head_dim
    tp_index = lax.axis_index("tp")
    ctx_index = lax.axis_index("ctx")
    ctx_count = lax.axis_size("ctx")
    local_x = tokens.astype(jnp.float32)
    kv_full = kv_weight
    if heads_dev == 1:
        partner = from_partner(kv_weight, "tp", 0)
        is_even = tp_index % 2 == 0
        kv_full = jnp.where(
            is_even,
            jnp.concatenate([kv_weight, partner], axis=2),
            jnp.concatenate([partner, kv_weight], axis=2),
        )
    gathered = lax.all_gather(tokens, "tp", axis=1, tiled=True).astype(jnp.float32)
    normed = rms_norm(gathered, input_gain).astype(jnp.bfloat16)
    query_raw = jnp.dot(normed, query_weight, preferred_element_type=jnp.float32)
    key_raw = jnp.dot(normed, kv_full[0], preferred_element_type=jnp.float32)
    value_raw = jnp.dot(normed, kv_full[1], preferred_element_type=jnp.float32)
    kv_heads = key_raw.shape[1] // head_dim
    group_size = heads_dev // kv_heads
    queries = (
        rotate(rms_norm(query_raw.reshape(tok_rows, heads_dev, head_dim), query_gain), positions)
        * (D // H) ** (-0.5)
    ).astype(jnp.bfloat16)
    keys = rotate(
        rms_norm(key_raw.reshape(tok_rows, kv_heads, head_dim), key_gain), positions
    ).astype(jnp.bfloat16)
    values_b = value_raw.reshape(tok_rows, kv_heads, head_dim).astype(jnp.bfloat16)
    kv_block = jnp.stack([keys, values_b])
    reach_blocks = min(ctx_count - 1, (WINDOW + tok_rows - 2) // tok_rows)
    received = []
    moving = kv_block
    for offset in range(reach_blocks):
        moving = passed_along(moving, "ctx", 1)
        received.append(moving)
    blocks = received[::-1] + [kv_block]
    keys_all = jnp.concatenate(blocks, axis=1)
    key_count = keys_all.shape[1]
    key_index = (ctx_index - reach_blocks) * tok_rows + jnp.arange(key_count, dtype=jnp.int32)
    query_index = ctx_index * tok_rows + jnp.arange(tok_rows, dtype=jnp.int32)
    visible = (key_index[None, :] >= first_key[:, None]) & (
        key_index[None, :] <= query_index[:, None]
    )
    grouped = queries.reshape(tok_rows, kv_heads, group_size, head_dim)
    scores = jnp.einsum("qkgd,tkd->kgqt", grouped, keys_all[0], preferred_element_type=jnp.float32)
    scores = jnp.where(visible[None, None], scores, -1e30)
    row_max = jnp.max(scores, axis=-1, keepdims=True)
    weights = jnp.exp(scores - row_max)
    denominator = jnp.sum(weights, axis=-1)
    mixed_out = jnp.einsum(
        "kgqt,tkd->qkgd",
        weights.astype(jnp.bfloat16),
        keys_all[1],
        preferred_element_type=jnp.float32,
    )
    mixed_out = mixed_out / jnp.transpose(denominator, (2, 0, 1))[..., None]
    attn = mixed_out.astype(jnp.bfloat16).reshape(tok_rows, heads_dev * head_dim)
    partial_value = jnp.dot(attn, out_weight, preferred_element_type=jnp.float32)
    summed = lax.psum(partial_value.astype(jnp.bfloat16), "tp").astype(jnp.float32)
    post_normed = rms_norm(summed, post_gain)
    own_cols = lax.dynamic_slice_in_dim(post_normed, tp_index * feat_dev, feat_dev, 1)
    return (local_x + own_cols).astype(jnp.bfloat16)


MESH = pl.DeviceIdType.MESH
F32 = jnp.float32
BF16 = jnp.bfloat16
TP = 4
CTX = 4
CHUNKS = 2
PRESCALE = 2.0**-10


def fused_kernel(
    tok_ref, pos_ref, fk_ref, ig_ref, qg_ref, kg_ref, pg_ref, qw_hbm, kvw_hbm, ow_hbm, out_ref,
    xbuf, xg_ref, gain_out, wq, wkv, wo, gain_in, gain_post, ssq_ref, kv_acc, q_acc, cos_ref, sin_ref,
    kvbuf, q_ref, m_ref, l_ref, o_ref, attn_ref, part, rup, rdn, own, sq_mine, sq_all,
    w_sem, wo_sem, ag_up, ag_dn, ag_recv, kv_send, kv_recv,
    rs_up_send, rs_dn_send, rs_up_recv, rs_dn_recv, sq_send, sq_recv,
):
    feat, rows = tok_ref.shape
    piece = feat // CHUNKS
    hd = qg_ref.shape[1]
    kv_heads = wkv.shape[2] // hd
    heads = wq.shape[1] // hd
    model = feat * TP
    z = lax.axis_index("tp")
    c = lax.axis_index("ctx")
    partner = c + 1 - 2 * (c % 2)
    far = lax.rem(c + 2, CTX)

    barrier = pltpu.get_barrier_semaphore()
    up = {"tp": lax.rem(z + 1, TP)}
    down = {"tp": lax.rem(z + TP - 1, TP)}

    @pl.when(z < TP - 1)
    def _():
        pl.semaphore_signal(barrier, inc=1, device_id=up, device_id_type=MESH)

    @pl.when(z > 0)
    def _():
        pl.semaphore_signal(barrier, inc=1, device_id=down, device_id_type=MESH)

    pl.semaphore_signal(barrier, inc=1, device_id={"ctx": partner}, device_id_type=MESH)
    pl.semaphore_signal(barrier, inc=1, device_id={"ctx": far}, device_id_type=MESH)
    def weight_span(src, ch):
        return pl.ds(pl.multiple_of(src * feat + ch * piece, 32), piece)

    def weight_copies(src, ch):
        span = weight_span(src, ch)
        return (
            pltpu.make_async_copy(kvw_hbm.at[0, span], wkv.at[0, span], w_sem.at[src, ch, 0]),
            pltpu.make_async_copy(kvw_hbm.at[1, span], wkv.at[1, span], w_sem.at[src, ch, 1]),
            pltpu.make_async_copy(qw_hbm.at[span], wq.at[span], w_sem.at[src, ch, 2]),
        )

    def each_source(fn):
        def at_distance(d, carry):
            @pl.when(z - d >= 0)
            def _():
                fn(z - d, d)

            @pl.when((z + d < TP) & (d > 0))
            def _():
                fn(z + d, d)

            return carry

        lax.fori_loop(0, TP, at_distance, 0)

    def begin_weights(src, d):
        for ch in range(CHUNKS):
            for copy in weight_copies(src, ch):
                copy.start()

    each_source(begin_weights)
    wo_copy = pltpu.make_async_copy(ow_hbm, wo, wo_sem)
    wo_copy.start()

    pl.semaphore_wait(barrier, jnp.where((z > 0) & (z < TP - 1), 4, 3))

    def piece_of(ch):
        return pl.ds(pl.multiple_of(ch * piece, 32), piece)

    def ag_copy(source, src, ch, send, target):
        return pltpu.make_async_remote_copy(
            src_ref=source,
            dst_ref=xbuf.at[src, piece_of(ch)],
            send_sem=send.at[src, ch],
            recv_sem=ag_recv.at[src, ch],
            device_id=target,
            device_id_type=MESH,
        )

    for ch in range(CHUNKS):
        @pl.when(z < TP - 1)
        def _():
            ag_copy(tok_ref.at[piece_of(ch)], z, ch, ag_up, up).start()

        @pl.when(z > 0)
        def _():
            ag_copy(tok_ref.at[piece_of(ch)], z, ch, ag_dn, down).start()

    gains = ig_ref[...].reshape(1, model) * PRESCALE
    post_gains = pg_ref[...].reshape(1, model)
    for i in range(TP * CHUNKS):
        gain_in[i] = gains[:, i * piece : (i + 1) * piece]
    for i in range(TP):
        gain_post[i] = post_gains[:, i * feat : (i + 1) * feat]
    xbuf[z] = tok_ref[...]
    ssq_ref[...] = jnp.zeros_like(ssq_ref)
    kv_acc[...] = jnp.zeros_like(kv_acc)
    q_acc[...] = jnp.zeros_like(q_acc)
    r_iota = lax.broadcasted_iota(jnp.int32, (rows, rows), 0)
    c_iota = lax.broadcasted_iota(jnp.int32, (rows, rows), 1)
    diagonal = r_iota == c_iota

    def as_column(row):
        return jnp.sum(jnp.where(diagonal, row, 0.0), axis=1, keepdims=True)

    lane = lax.broadcasted_iota(jnp.int32, (rows, hd), 1)
    half = jnp.where(lane < hd // 2, lane, lane - hd // 2).astype(F32)
    angles = as_column(pos_ref[...].astype(F32)) * jnp.exp(half * (-2.0 * math.log(10000.0) / hd))
    cos_ref[...] = jnp.cos(angles)
    sines = jnp.sin(angles)
    sin_ref[...] = jnp.where(lane < hd // 2, -sines, sines)
    gain_out[...] = jnp.broadcast_to(gain_post[z], (rows, feat)).T
    first = as_column(fk_ref[...].astype(F32)).astype(jnp.int32)

    last = jnp.where(z < TP // 2, TP - 1, 0)

    def query_product(src, ch):
        weight_copies(src, ch)[2].wait()
        q_acc[...] += jnp.dot(
            xg_ref[...], wq[weight_span(src, ch)], preferred_element_type=F32
        )

    def projections(src, ch):
        x_t = xbuf[src, piece_of(ch)].astype(F32)
        ssq_ref[...] += jnp.sum(x_t * x_t, axis=0, keepdims=True)
        xg_ref[...] = (x_t.T * gain_in[src * CHUNKS + ch]).astype(BF16)
        width = wkv.shape[2]
        for i in range(2):
            weight_copies(src, ch)[i].wait()
            kv_acc[:, i * width : (i + 1) * width] += jnp.dot(
                xg_ref[...], wkv[i, weight_span(src, ch)], preferred_element_type=F32
            )

        @pl.when((src != last) | (ch < CHUNKS - 1))
        def _():
            query_product(src, ch)

    def gather_step(k, carry):
        d = k // CHUNKS
        ch = k % CHUNKS
        low = z - d
        high = z + d

        @pl.when((d > 0) & (low >= 0))
        def _():
            here = xbuf.at[low, piece_of(ch)]
            ag_copy(here, low, ch, ag_up, down).wait_recv()

            @pl.when(z < TP - 1)
            def _():
                ag_copy(here, low, ch, ag_up, up).start()

        @pl.when((d > 0) & (high < TP))
        def _():
            here = xbuf.at[high, piece_of(ch)]
            ag_copy(here, high, ch, ag_dn, up).wait_recv()

            @pl.when(z > 0)
            def _():
                ag_copy(here, high, ch, ag_dn, down).start()

        def side(i, inner):
            src = jnp.where(i == 0, low, high)

            @pl.when((src >= 0) & (src < TP) & ((d > 0) | (i == 0)))
            def _():
                projections(src, ch)

            return inner

        lax.fori_loop(0, 2, side, 0)
        return carry

    lax.fori_loop(0, TP * CHUNKS, gather_step, 0)

    inv = lax.rsqrt(as_column(ssq_ref[...]) * (1.0 / model) + EPSILON) * (1.0 / PRESCALE)

    def normed_rotated(raw, gain_vec):
        raw = raw * inv
        scaled = raw * lax.rsqrt(jnp.mean(raw * raw, axis=1, keepdims=True) + EPSILON) * gain_vec
        return scaled * cos_ref[...] + pltpu.roll(scaled, hd // 2, 1) * sin_ref[...]

    width = kv_heads * hd
    for h in range(kv_heads):
        cols = slice(h * hd, (h + 1) * hd)
        kvbuf[c, 0, :, cols] = normed_rotated(kv_acc[:, cols], kg_ref[...]).astype(BF16)
    kvbuf[c, 1] = (kv_acc[:, width:] * inv).astype(BF16)

    def kv_copy(block, step, target):
        return pltpu.make_async_remote_copy(
            src_ref=kvbuf.at[block],
            dst_ref=kvbuf.at[block],
            send_sem=kv_send.at[step],
            recv_sem=kv_recv.at[step],
            device_id={"ctx": target},
            device_id_type=MESH,
        )

    @pl.when(c < CTX // 2)
    def _():
        kv_copy(c, 1, far).start()

    @pl.when(c % 2 == 0)
    def _():
        kv_copy(c, 0, partner).start()

    query_product(last, CHUNKS - 1)
    for h in range(heads):
        cols = slice(h * hd, (h + 1) * hd)
        spot = slice((h % 2) * rows, (h % 2 + 1) * rows)
        q_ref[h // 2, spot] = (
            normed_rotated(q_acc[:, cols], qg_ref[...]) * (D // H) ** (-0.5)
        ).astype(BF16)

    m_ref[...] = jnp.full_like(m_ref, -1e30)
    l_ref[...] = jnp.zeros_like(l_ref)
    o_ref[...] = jnp.zeros_like(o_ref)

    def attend(block):
        key_index = block * rows + c_iota
        visible = (key_index >= first) & (key_index <= c * rows + r_iota)
        bias = jnp.where(visible, 0.0, -1e30)
        bias = jnp.concatenate([bias, bias], axis=0)
        for h in range(kv_heads):
            cols = slice(h * hd, (h + 1) * hd)
            s = lax.dot_general(
                q_ref[h], kvbuf[block, 0, :, cols], (((1,), (1,)), ((), ())),
                preferred_element_type=F32,
            )
            s = jnp.where(bias < 0.0, -1e30, s)
            old = m_ref[h]
            new = jnp.maximum(old, jnp.max(s, axis=1, keepdims=True))
            fade = jnp.exp(old - new)
            p = jnp.exp(s - new)
            m_ref[h] = new
            l_ref[h] = l_ref[h] * fade + jnp.sum(p, axis=1, keepdims=True)
            o_ref[h] = o_ref[h] * fade + jnp.dot(
                p.astype(BF16), kvbuf[block, 1, :, cols], preferred_element_type=F32
            )

    def attention_step(step, carry):
        block = jnp.where(
            step == 0, c, jnp.where(step == 1, c - 1, jnp.where(step == 2, c - 2, partner - 2))
        )
        valid = (step == 0) | ((step == 1) & (c % 2 == 1)) | ((step >= 2) & (c >= CTX // 2))

        @pl.when(valid)
        def _():
            @pl.when(step > 0)
            def _():
                kv_copy(block, step - 1, partner).wait_recv()

            @pl.when(step == 2)
            def _():
                kv_copy(block, 2, partner).start()

            attend(block)

        return carry

    lax.fori_loop(0, CTX, attention_step, 0)

    for h in range(heads):
        spot = slice((h % 2) * rows, (h % 2 + 1) * rows)
        attn_ref[:, h * hd : (h + 1) * hd] = (
            o_ref[h // 2, spot] / l_ref[h // 2, spot]
        ).astype(BF16)

    wo_copy.wait()

    def rs_copy(dest, ch, buf, send, recv, target):
        return pltpu.make_async_remote_copy(
            src_ref=part.at[dest, piece_of(ch)],
            dst_ref=buf.at[dest, piece_of(ch)],
            send_sem=send.at[dest, ch],
            recv_sem=recv.at[dest, ch],
            device_id=target,
            device_id_type=MESH,
        )

    def rs_up(dest, ch):
        return rs_copy(dest, ch, rup, rs_up_send, rs_up_recv, up)

    def rs_dn(dest, ch):
        return rs_copy(dest, ch, rdn, rs_dn_send, rs_dn_recv, down)

    shift = feat % 128
    wide = feat + shift

    def out_step(k, carry):
        outer = TP - 1 - k
        inner = jnp.where(k == 0, 3, jnp.where(k == 1, 0, jnp.where(k == 2, 2, 1)))
        edge = (z == 0) | (z == TP - 1)
        dest = jnp.where(edge, outer, inner)
        dest = jnp.where(z < TP // 2, dest, TP - 1 - dest)
        odd = dest % 2
        start = pl.multiple_of((dest // 2) * (2 * feat) + odd * (feat - shift), 128)
        term = jnp.dot(
            attn_ref[...], wo[:, pl.ds(start, wide)], preferred_element_type=F32
        ).T.astype(BF16)

        @pl.when(odd == 0)
        def _():
            part[dest] = term[:feat]

        @pl.when(odd == 1)
        def _():
            part[dest] = term[shift:]

        for ch in range(CHUNKS):
            @pl.when((z == 0) & (dest > 0))
            def _():
                rs_up(dest, ch).start()

            @pl.when((z == TP - 1) & (dest < TP - 1))
            def _():
                rs_dn(dest, ch).start()

        return carry

    lax.fori_loop(0, TP, out_step, 0)
    own[...] = part[z].astype(F32)

    def sum_step(k, carry):
        for ch in range(CHUNKS):
            span = piece_of(ch)
            from_low = z + TP - 1 - k
            from_high = z + k - (TP - 1)
            for dest, has, buf, copy in (
                (from_low, (z > 0) & (from_low < TP), rup, rs_up),
                (from_high, (z < TP - 1) & (from_high >= 0), rdn, rs_dn),
            ):
                @pl.when(has)
                def _():
                    copy(dest, ch).wait_recv()

                    @pl.when(dest != z)
                    def _():
                        part[dest, span] = (
                            part[dest, span].astype(F32) + buf[dest, span].astype(F32)
                        ).astype(BF16)
                        copy(dest, ch).start()

                    @pl.when(dest == z)
                    def _():
                        own[span] += buf[dest, span].astype(F32)

        return carry

    lax.fori_loop(1, TP, sum_step, 0)

    as_row = jnp.sum(own[...] * own[...], axis=0, keepdims=True)
    sq_mine[...] = jnp.broadcast_to(as_row, sq_mine.shape)

    def sq_copy(d, slot):
        return pltpu.make_async_remote_copy(
            src_ref=sq_mine,
            dst_ref=sq_all.at[slot],
            send_sem=sq_send.at[d],
            recv_sem=sq_recv.at[slot],
            device_id={"tp": lax.rem(z + d, TP)},
            device_id_type=MESH,
        )

    for d in range(1, TP):
        sq_copy(d, z).start()
    for d in range(1, TP):
        slot = lax.rem(z + d, TP)
        sq_copy(d, slot).wait_recv()
        as_row = as_row + sq_all[slot, 0:1]
    inv_post = lax.rsqrt(as_row * (1.0 / model) + EPSILON)
    out_ref[...] = (
        tok_ref[...].astype(F32) + own[...] * inv_post * gain_out[...]
    ).astype(BF16)

    for d in range(1, TP):
        sq_copy(d, z).wait_send()

    def settle(i, carry):
        for ch in range(CHUNKS):
            @pl.when((z < TP - 1) & (i <= z))
            def _():
                ag_copy(xbuf.at[i, piece_of(ch)], i, ch, ag_up, up).wait_send()

            @pl.when((z > 0) & (i >= z))
            def _():
                ag_copy(xbuf.at[i, piece_of(ch)], i, ch, ag_dn, down).wait_send()

            @pl.when(i > z)
            def _():
                rs_up(i, ch).wait_send()

            @pl.when(i < z)
            def _():
                rs_dn(i, ch).wait_send()

        return carry

    lax.fori_loop(0, TP, settle, 0)

    @pl.when(c < CTX // 2)
    def _():
        kv_copy(c, 1, far).wait_send()

    @pl.when(c % 2 == 0)
    def _():
        kv_copy(c, 0, partner).wait_send()

    @pl.when(c >= CTX // 2)
    def _():
        kv_copy(c - 2, 2, partner).wait_send()


def per_device_fused(
    tokens, positions, first_key, input_gain, query_weight, kv_weight, query_gain, key_gain,
    out_weight, post_gain,
):
    feat, rows = tokens.shape[1], tokens.shape[0]
    piece = feat // CHUNKS
    hd = query_gain.shape[0]
    q_cols = query_weight.shape[1]
    kv_cols = kv_weight.shape[2]
    model = query_weight.shape[0]
    kv_heads = kv_cols // hd
    vmem = pl.BlockSpec(memory_space=pltpu.VMEM)
    anywhere = pl.BlockSpec(memory_space=pl.ANY)
    dma = pltpu.SemaphoreType.DMA
    state = (kv_heads, 2 * rows, hd)
    return pl.pallas_call(
        fused_kernel,
        out_shape=jax.ShapeDtypeStruct((feat, rows), BF16),
        in_specs=[vmem] * 7 + [anywhere] * 3,
        out_specs=vmem,
        scratch_shapes=[
            pltpu.VMEM((TP, feat, rows), BF16),
            pltpu.VMEM((rows, piece), BF16),
            pltpu.VMEM((feat, rows), F32),
            pltpu.VMEM((model, q_cols), BF16),
            pltpu.VMEM((2, model, kv_cols), BF16),
            pltpu.VMEM((q_cols, model), BF16),
            pltpu.VMEM((TP * CHUNKS, 1, piece), F32),
            pltpu.VMEM((TP, 1, feat), F32),
            pltpu.VMEM((1, rows), F32),
            pltpu.VMEM((rows, 2 * kv_cols), F32),
            pltpu.VMEM((rows, q_cols), F32),
            pltpu.VMEM((rows, hd), F32),
            pltpu.VMEM((rows, hd), F32),
            pltpu.VMEM((CTX, 2, rows, kv_cols), BF16),
            pltpu.VMEM(state, BF16),
            pltpu.VMEM((kv_heads, 2 * rows, 1), F32),
            pltpu.VMEM((kv_heads, 2 * rows, 1), F32),
            pltpu.VMEM(state, F32),
            pltpu.VMEM((rows, q_cols), BF16),
            pltpu.VMEM((TP, feat, rows), BF16),
            pltpu.VMEM((TP, feat, rows), BF16),
            pltpu.VMEM((TP, feat, rows), BF16),
            pltpu.VMEM((feat, rows), F32),
            pltpu.VMEM((8, rows), F32),
            pltpu.VMEM((TP, 8, rows), F32),
            dma((TP, CHUNKS, 3)),
            dma,
            dma((TP, CHUNKS)),
            dma((TP, CHUNKS)),
            dma((TP, CHUNKS)),
            dma((3,)),
            dma((3,)),
            dma((TP, CHUNKS)),
            dma((TP, CHUNKS)),
            dma((TP, CHUNKS)),
            dma((TP, CHUNKS)),
            dma((TP,)),
            dma((TP,)),
        ],
        compiler_params=pltpu.CompilerParams(
            collective_id=0, has_side_effects=True, vmem_limit_bytes=60 * 1024 * 1024
        ),
    )(
        tokens.T,
        positions.reshape(1, rows),
        first_key.reshape(1, rows),
        input_gain,
        query_gain.reshape(1, hd),
        key_gain.reshape(1, hd),
        post_gain,
        query_weight,
        kv_weight,
        out_weight,
    ).T


def solution(mesh):
    fused = mesh.shape["tp"] == TP and mesh.shape["ctx"] == CTX
    return jax.shard_map(
        per_device_fused if fused else per_device,
        mesh=mesh,
        in_specs=(
            P(("group", "ctx"), "tp"),
            P(("group", "ctx")),
            P(("group", "ctx")),
            P(),
            P(None, "tp"),
            P(None, None, "tp"),
            P(),
            P(),
            P("tp", None),
            P(),
        ),
        out_specs=P(("group", "ctx"), "tp"),
        check_vma=False,
    )
```

```python
import math

import jax
import jax.numpy as jnp
from jax import lax
from jax.experimental import pallas as pl
from jax.experimental.pallas import tpu as pltpu
from jax.sharding import PartitionSpec as P

D = 5376
H = 32
WINDOW = 1024


EPSILON = 1e-06


def from_partner(array, axis, distance):
    return lax.ppermute(array, axis, [(i, i ^ 1 << distance) for i in range(lax.axis_size(axis))])


def passed_along(block, axis, distance):
    devices = range(lax.axis_size(axis))
    route = [(i - distance, i) for i in devices if i - distance in devices]
    return lax.ppermute(block, axis, route)


def rms_norm(values, gain_vec):
    return (
        values * lax.rsqrt(jnp.mean(values * values, axis=-1, keepdims=True) + EPSILON) * gain_vec
    )


def rotate(values, positions_in):
    half_dim = values.shape[-1] // 2
    frequency = jnp.exp(
        jnp.arange(half_dim, dtype=jnp.float32) * (-2.0 * math.log(10000.0) / values.shape[-1])
    )
    angles = positions_in.astype(jnp.float32)[:, None] * frequency[None, :]
    cosines = jnp.cos(angles)[:, None, :]
    sine_part = jnp.sin(angles)[:, None, :]
    lower_half = values[..., :half_dim]
    upper_half = values[..., half_dim:]
    return jnp.concatenate(
        [
            lower_half * cosines - upper_half * sine_part,
            upper_half * cosines + lower_half * sine_part,
        ],
        axis=-1,
    )


def per_device(
    tokens,
    positions,
    first_key,
    input_gain,
    query_weight,
    kv_weight,
    query_gain,
    key_gain,
    out_weight,
    post_gain,
):
    tok_rows = tokens.shape[0]
    feat_dev = tokens.shape[1]
    head_dim = query_gain.shape[0]
    heads_dev = query_weight.shape[1] // head_dim
    tp_index = lax.axis_index("tp")
    ctx_index = lax.axis_index("ctx")
    ctx_count = lax.axis_size("ctx")
    local_x = tokens.astype(jnp.float32)
    kv_full = kv_weight
    if heads_dev == 1:
        partner = from_partner(kv_weight, "tp", 0)
        is_even = tp_index % 2 == 0
        kv_full = jnp.where(
            is_even,
            jnp.concatenate([kv_weight, partner], axis=2),
            jnp.concatenate([partner, kv_weight], axis=2),
        )
    gathered = lax.all_gather(tokens, "tp", axis=1, tiled=True).astype(jnp.float32)
    normed = rms_norm(gathered, input_gain).astype(jnp.bfloat16)
    query_raw = jnp.dot(normed, query_weight, preferred_element_type=jnp.float32)
    key_raw = jnp.dot(normed, kv_full[0], preferred_element_type=jnp.float32)
    value_raw = jnp.dot(normed, kv_full[1], preferred_element_type=jnp.float32)
    kv_heads = key_raw.shape[1] // head_dim
    group_size = heads_dev // kv_heads
    queries = (
        rotate(rms_norm(query_raw.reshape(tok_rows, heads_dev, head_dim), query_gain), positions)
        * (D // H) ** (-0.5)
    ).astype(jnp.bfloat16)
    keys = rotate(
        rms_norm(key_raw.reshape(tok_rows, kv_heads, head_dim), key_gain), positions
    ).astype(jnp.bfloat16)
    values_b = value_raw.reshape(tok_rows, kv_heads, head_dim).astype(jnp.bfloat16)
    kv_block = jnp.stack([keys, values_b])
    reach_blocks = min(ctx_count - 1, (WINDOW + tok_rows - 2) // tok_rows)
    received = []
    moving = kv_block
    for offset in range(reach_blocks):
        moving = passed_along(moving, "ctx", 1)
        received.append(moving)
    blocks = received[::-1] + [kv_block]
    keys_all = jnp.concatenate(blocks, axis=1)
    key_count = keys_all.shape[1]
    key_index = (ctx_index - reach_blocks) * tok_rows + jnp.arange(key_count, dtype=jnp.int32)
    query_index = ctx_index * tok_rows + jnp.arange(tok_rows, dtype=jnp.int32)
    visible = (key_index[None, :] >= first_key[:, None]) & (
        key_index[None, :] <= query_index[:, None]
    )
    grouped = queries.reshape(tok_rows, kv_heads, group_size, head_dim)
    scores = jnp.einsum("qkgd,tkd->kgqt", grouped, keys_all[0], preferred_element_type=jnp.float32)
    scores = jnp.where(visible[None, None], scores, -1e30)
    row_max = jnp.max(scores, axis=-1, keepdims=True)
    weights = jnp.exp(scores - row_max)
    denominator = jnp.sum(weights, axis=-1)
    mixed_out = jnp.einsum(
        "kgqt,tkd->qkgd",
        weights.astype(jnp.bfloat16),
        keys_all[1],
        preferred_element_type=jnp.float32,
    )
    mixed_out = mixed_out / jnp.transpose(denominator, (2, 0, 1))[..., None]
    attn = mixed_out.astype(jnp.bfloat16).reshape(tok_rows, heads_dev * head_dim)
    partial_value = jnp.dot(attn, out_weight, preferred_element_type=jnp.float32)
    summed = lax.psum(partial_value.astype(jnp.bfloat16), "tp").astype(jnp.float32)
    post_normed = rms_norm(summed, post_gain)
    own_cols = lax.dynamic_slice_in_dim(post_normed, tp_index * feat_dev, feat_dev, 1)
    return (local_x + own_cols).astype(jnp.bfloat16)


MESH = pl.DeviceIdType.MESH
F32 = jnp.float32
BF16 = jnp.bfloat16
TP = 4
CTX = 4
CHUNKS = 2
PRESCALE = 2.0**-10


def fused_kernel(
    tok_ref, pos_ref, fk_ref, ig_ref, qg_ref, kg_ref, pg_ref, qw_hbm, kvw_hbm, ow_hbm, out_ref,
    xbuf, xg_ref, gain_out, wq, wkv, wo, gain_in, gain_post, ssq_ref, kv_acc, q_acc, cos_ref, sin_ref,
    kvbuf, q_ref, m_ref, l_ref, o_ref, attn_ref, part, rup, rdn, own, sq_mine, sq_all,
    w_sem, wo_sem, ag_up, ag_dn, ag_recv, kv_send, kv_recv,
    rs_up_send, rs_dn_send, rs_up_recv, rs_dn_recv, sq_send, sq_recv,
):
    feat, rows = tok_ref.shape
    piece = feat // CHUNKS
    hd = qg_ref.shape[1]
    kv_heads = wkv.shape[2] // hd
    heads = wq.shape[1] // hd
    model = feat * TP
    z = lax.axis_index("tp")
    c = lax.axis_index("ctx")
    partner = c + 1 - 2 * (c % 2)
    far = lax.rem(c + 2, CTX)

    barrier = pltpu.get_barrier_semaphore()
    up = {"tp": lax.rem(z + 1, TP)}
    down = {"tp": lax.rem(z + TP - 1, TP)}

    @pl.when(z < TP - 1)
    def _():
        pl.semaphore_signal(barrier, inc=1, device_id=up, device_id_type=MESH)

    @pl.when(z > 0)
    def _():
        pl.semaphore_signal(barrier, inc=1, device_id=down, device_id_type=MESH)

    pl.semaphore_signal(barrier, inc=1, device_id={"ctx": partner}, device_id_type=MESH)
    pl.semaphore_signal(barrier, inc=1, device_id={"ctx": far}, device_id_type=MESH)
    def weight_span(src, ch):
        return pl.ds(pl.multiple_of(src * feat + ch * piece, 32), piece)

    def weight_copies(src, ch):
        span = weight_span(src, ch)
        return (
            pltpu.make_async_copy(kvw_hbm.at[0, span], wkv.at[0, span], w_sem.at[src, ch, 0]),
            pltpu.make_async_copy(kvw_hbm.at[1, span], wkv.at[1, span], w_sem.at[src, ch, 1]),
            pltpu.make_async_copy(qw_hbm.at[span], wq.at[span], w_sem.at[src, ch, 2]),
        )

    def each_source(fn):
        def at_distance(d, carry):
            @pl.when(z - d >= 0)
            def _():
                fn(z - d, d)

            @pl.when((z + d < TP) & (d > 0))
            def _():
                fn(z + d, d)

            return carry

        lax.fori_loop(0, TP, at_distance, 0)

    def begin_weights(src, d):
        for ch in range(CHUNKS):
            for copy in weight_copies(src, ch):
                copy.start()

    each_source(begin_weights)
    wo_copy = pltpu.make_async_copy(ow_hbm, wo, wo_sem)
    wo_copy.start()

    pl.semaphore_wait(barrier, jnp.where((z > 0) & (z < TP - 1), 4, 3))

    def piece_of(ch):
        return pl.ds(pl.multiple_of(ch * piece, 32), piece)

    def ag_copy(source, src, ch, send, target):
        return pltpu.make_async_remote_copy(
            src_ref=source,
            dst_ref=xbuf.at[src, piece_of(ch)],
            send_sem=send.at[src, ch],
            recv_sem=ag_recv.at[src, ch],
            device_id=target,
            device_id_type=MESH,
        )

    for ch in range(CHUNKS):
        @pl.when(z < TP - 1)
        def _():
            ag_copy(tok_ref.at[piece_of(ch)], z, ch, ag_up, up).start()

        @pl.when(z > 0)
        def _():
            ag_copy(tok_ref.at[piece_of(ch)], z, ch, ag_dn, down).start()

    gains = ig_ref[...].reshape(1, model) * PRESCALE
    post_gains = pg_ref[...].reshape(1, model)
    for i in range(TP * CHUNKS):
        gain_in[i] = gains[:, i * piece : (i + 1) * piece]
    for i in range(TP):
        gain_post[i] = post_gains[:, i * feat : (i + 1) * feat]
    xbuf[z] = tok_ref[...]
    ssq_ref[...] = jnp.zeros_like(ssq_ref)
    kv_acc[...] = jnp.zeros_like(kv_acc)
    q_acc[...] = jnp.zeros_like(q_acc)
    r_iota = lax.broadcasted_iota(jnp.int32, (rows, rows), 0)
    c_iota = lax.broadcasted_iota(jnp.int32, (rows, rows), 1)
    diagonal = r_iota == c_iota

    def as_column(row):
        return jnp.sum(jnp.where(diagonal, row, 0.0), axis=1, keepdims=True)

    lane = lax.broadcasted_iota(jnp.int32, (rows, hd), 1)
    half = jnp.where(lane < hd // 2, lane, lane - hd // 2).astype(F32)
    angles = as_column(pos_ref[...].astype(F32)) * jnp.exp(half * (-2.0 * math.log(10000.0) / hd))
    cos_ref[...] = jnp.cos(angles)
    sines = jnp.sin(angles)
    sin_ref[...] = jnp.where(lane < hd // 2, -sines, sines)
    gain_out[...] = jnp.broadcast_to(gain_post[z], (rows, feat)).T
    first = as_column(fk_ref[...].astype(F32)).astype(jnp.int32)

    last = jnp.where(z < TP // 2, TP - 1, 0)

    def query_product(src, ch):
        weight_copies(src, ch)[2].wait()
        q_acc[...] += jnp.dot(
            xg_ref[...], wq[weight_span(src, ch)], preferred_element_type=F32
        )

    def projections(src, ch):
        x_t = xbuf[src, piece_of(ch)].astype(F32)
        ssq_ref[...] += jnp.sum(x_t * x_t, axis=0, keepdims=True)
        xg_ref[...] = (x_t.T * gain_in[src * CHUNKS + ch]).astype(BF16)
        width = wkv.shape[2]
        for i in range(2):
            weight_copies(src, ch)[i].wait()
            kv_acc[:, i * width : (i + 1) * width] += jnp.dot(
                xg_ref[...], wkv[i, weight_span(src, ch)], preferred_element_type=F32
            )

        @pl.when((src != last) | (ch < CHUNKS - 1))
        def _():
            query_product(src, ch)

    def gather_step(k, carry):
        d = k // CHUNKS
        ch = k % CHUNKS
        low = z - d
        high = z + d

        @pl.when((d > 0) & (low >= 0))
        def _():
            here = xbuf.at[low, piece_of(ch)]
            ag_copy(here, low, ch, ag_up, down).wait_recv()

            @pl.when(z < TP - 1)
            def _():
                ag_copy(here, low, ch, ag_up, up).start()

        @pl.when((d > 0) & (high < TP))
        def _():
            here = xbuf.at[high, piece_of(ch)]
            ag_copy(here, high, ch, ag_dn, up).wait_recv()

            @pl.when(z > 0)
            def _():
                ag_copy(here, high, ch, ag_dn, down).start()

        def side(i, inner):
            src = jnp.where(i == 0, low, high)

            @pl.when((src >= 0) & (src < TP) & ((d > 0) | (i == 0)))
            def _():
                projections(src, ch)

            return inner

        lax.fori_loop(0, 2, side, 0)
        return carry

    lax.fori_loop(0, TP * CHUNKS, gather_step, 0)

    inv = lax.rsqrt(as_column(ssq_ref[...]) * (1.0 / model) + EPSILON) * (1.0 / PRESCALE)

    def normed_rotated(raw, gain_vec):
        raw = raw * inv
        scaled = raw * lax.rsqrt(jnp.mean(raw * raw, axis=1, keepdims=True) + EPSILON) * gain_vec
        return scaled * cos_ref[...] + pltpu.roll(scaled, hd // 2, 1) * sin_ref[...]

    width = kv_heads * hd
    for h in range(kv_heads):
        cols = slice(h * hd, (h + 1) * hd)
        kvbuf[c, 0, :, cols] = normed_rotated(kv_acc[:, cols], kg_ref[...]).astype(BF16)
    kvbuf[c, 1] = (kv_acc[:, width:] * inv).astype(BF16)

    def kv_copy(block, step, target):
        return pltpu.make_async_remote_copy(
            src_ref=kvbuf.at[block],
            dst_ref=kvbuf.at[block],
            send_sem=kv_send.at[step],
            recv_sem=kv_recv.at[step],
            device_id={"ctx": target},
            device_id_type=MESH,
        )

    @pl.when(c < CTX // 2)
    def _():
        kv_copy(c, 1, far).start()

    @pl.when(c % 2 == 0)
    def _():
        kv_copy(c, 0, partner).start()

    query_product(last, CHUNKS - 1)
    for h in range(heads):
        cols = slice(h * hd, (h + 1) * hd)
        spot = slice((h % 2) * rows, (h % 2 + 1) * rows)
        q_ref[h // 2, spot] = (
            normed_rotated(q_acc[:, cols], qg_ref[...]) * (D // H) ** (-0.5)
        ).astype(BF16)

    m_ref[...] = jnp.full_like(m_ref, -1e30)
    l_ref[...] = jnp.zeros_like(l_ref)
    o_ref[...] = jnp.zeros_like(o_ref)

    def attend(block):
        key_index = block * rows + c_iota
        visible = (key_index >= first) & (key_index <= c * rows + r_iota)
        bias = jnp.where(visible, 0.0, -1e30)
        bias = jnp.concatenate([bias, bias], axis=0)
        for h in range(kv_heads):
            cols = slice(h * hd, (h + 1) * hd)
            s = lax.dot_general(
                q_ref[h], kvbuf[block, 0, :, cols], (((1,), (1,)), ((), ())),
                preferred_element_type=F32,
            )
            s = jnp.where(bias < 0.0, -1e30, s)
            old = m_ref[h]
            new = jnp.maximum(old, jnp.max(s, axis=1, keepdims=True))
            fade = jnp.exp(old - new)
            p = jnp.exp(s - new)
            m_ref[h] = new
            l_ref[h] = l_ref[h] * fade + jnp.sum(p, axis=1, keepdims=True)
            o_ref[h] = o_ref[h] * fade + jnp.dot(
                p.astype(BF16), kvbuf[block, 1, :, cols], preferred_element_type=F32
            )

    def attention_step(step, carry):
        block = jnp.where(
            step == 0, c, jnp.where(step == 1, c - 1, jnp.where(step == 2, c - 2, partner - 2))
        )
        valid = (step == 0) | ((step == 1) & (c % 2 == 1)) | ((step >= 2) & (c >= CTX // 2))

        @pl.when(valid)
        def _():
            @pl.when(step > 0)
            def _():
                kv_copy(block, step - 1, partner).wait_recv()

            @pl.when(step == 2)
            def _():
                kv_copy(block, 2, partner).start()

            attend(block)

        return carry

    lax.fori_loop(0, CTX, attention_step, 0)

    for h in range(heads):
        spot = slice((h % 2) * rows, (h % 2 + 1) * rows)
        attn_ref[:, h * hd : (h + 1) * hd] = (
            o_ref[h // 2, spot] / l_ref[h // 2, spot]
        ).astype(BF16)

    wo_copy.wait()

    def rs_copy(dest, ch, buf, send, recv, target):
        return pltpu.make_async_remote_copy(
            src_ref=part.at[dest, piece_of(ch)],
            dst_ref=buf.at[dest, piece_of(ch)],
            send_sem=send.at[dest, ch],
            recv_sem=recv.at[dest, ch],
            device_id=target,
            device_id_type=MESH,
        )

    def rs_up(dest, ch):
        return rs_copy(dest, ch, rup, rs_up_send, rs_up_recv, up)

    def rs_dn(dest, ch):
        return rs_copy(dest, ch, rdn, rs_dn_send, rs_dn_recv, down)

    extra = piece % 128
    turns = 128 // extra
    wide = piece + 128 - extra

    def out_step(step, carry):
        k = step // CHUNKS
        ch = step % CHUNKS
        outer = TP - 1 - k
        inner = jnp.where(k == 0, 3, jnp.where(k == 1, 0, jnp.where(k == 2, 2, 1)))
        edge = (z == 0) | (z == TP - 1)
        dest = jnp.where(edge, outer, inner)
        dest = jnp.where(z < TP // 2, dest, TP - 1 - dest)
        spot = dest * CHUNKS + ch
        turn = spot % turns
        start = pl.multiple_of(spot * piece - turn * extra, 128)
        term = jnp.dot(
            attn_ref[...], wo[:, pl.ds(start, wide)], preferred_element_type=F32
        ).T.astype(BF16)
        for i in range(turns):
            @pl.when(turn == i)
            def _():
                part[dest, piece_of(ch)] = term[i * extra : i * extra + piece]

        @pl.when((z == 0) & (dest > 0))
        def _():
            rs_up(dest, ch).start()

        @pl.when((z == TP - 1) & (dest < TP - 1))
        def _():
            rs_dn(dest, ch).start()

        return carry

    lax.fori_loop(0, TP * CHUNKS, out_step, 0)
    own[...] = part[z].astype(F32)

    def sum_step(k, carry):
        for ch in range(CHUNKS):
            span = piece_of(ch)
            from_low = z + TP - 1 - k
            from_high = z + k - (TP - 1)
            for dest, has, buf, copy in (
                (from_low, (z > 0) & (from_low < TP), rup, rs_up),
                (from_high, (z < TP - 1) & (from_high >= 0), rdn, rs_dn),
            ):
                @pl.when(has)
                def _():
                    copy(dest, ch).wait_recv()

                    @pl.when(dest != z)
                    def _():
                        part[dest, span] = (
                            part[dest, span].astype(F32) + buf[dest, span].astype(F32)
                        ).astype(BF16)
                        copy(dest, ch).start()

                    @pl.when(dest == z)
                    def _():
                        own[span] += buf[dest, span].astype(F32)

        return carry

    lax.fori_loop(1, TP, sum_step, 0)

    as_row = jnp.sum(own[...] * own[...], axis=0, keepdims=True)
    sq_mine[...] = jnp.broadcast_to(as_row, sq_mine.shape)

    def sq_copy(d, slot):
        return pltpu.make_async_remote_copy(
            src_ref=sq_mine,
            dst_ref=sq_all.at[slot],
            send_sem=sq_send.at[d],
            recv_sem=sq_recv.at[slot],
            device_id={"tp": lax.rem(z + d, TP)},
            device_id_type=MESH,
        )

    for d in range(1, TP):
        sq_copy(d, z).start()
    for d in range(1, TP):
        slot = lax.rem(z + d, TP)
        sq_copy(d, slot).wait_recv()
        as_row = as_row + sq_all[slot, 0:1]
    inv_post = lax.rsqrt(as_row * (1.0 / model) + EPSILON)
    out_ref[...] = (
        tok_ref[...].astype(F32) + own[...] * inv_post * gain_out[...]
    ).astype(BF16)

    for d in range(1, TP):
        sq_copy(d, z).wait_send()

    def settle(i, carry):
        for ch in range(CHUNKS):
            @pl.when((z < TP - 1) & (i <= z))
            def _():
                ag_copy(xbuf.at[i, piece_of(ch)], i, ch, ag_up, up).wait_send()

            @pl.when((z > 0) & (i >= z))
            def _():
                ag_copy(xbuf.at[i, piece_of(ch)], i, ch, ag_dn, down).wait_send()

            @pl.when(i > z)
            def _():
                rs_up(i, ch).wait_send()

            @pl.when(i < z)
            def _():
                rs_dn(i, ch).wait_send()

        return carry

    lax.fori_loop(0, TP, settle, 0)

    @pl.when(c < CTX // 2)
    def _():
        kv_copy(c, 1, far).wait_send()

    @pl.when(c % 2 == 0)
    def _():
        kv_copy(c, 0, partner).wait_send()

    @pl.when(c >= CTX // 2)
    def _():
        kv_copy(c - 2, 2, partner).wait_send()


def per_device_fused(
    tokens, positions, first_key, input_gain, query_weight, kv_weight, query_gain, key_gain,
    out_weight, post_gain,
):
    feat, rows = tokens.shape[1], tokens.shape[0]
    piece = feat // CHUNKS
    hd = query_gain.shape[0]
    q_cols = query_weight.shape[1]
    kv_cols = kv_weight.shape[2]
    model = query_weight.shape[0]
    kv_heads = kv_cols // hd
    vmem = pl.BlockSpec(memory_space=pltpu.VMEM)
    anywhere = pl.BlockSpec(memory_space=pl.ANY)
    dma = pltpu.SemaphoreType.DMA
    state = (kv_heads, 2 * rows, hd)
    return pl.pallas_call(
        fused_kernel,
        out_shape=jax.ShapeDtypeStruct((feat, rows), BF16),
        in_specs=[vmem] * 7 + [anywhere] * 3,
        out_specs=vmem,
        scratch_shapes=[
            pltpu.VMEM((TP, feat, rows), BF16),
            pltpu.VMEM((rows, piece), BF16),
            pltpu.VMEM((feat, rows), F32),
            pltpu.VMEM((model, q_cols), BF16),
            pltpu.VMEM((2, model, kv_cols), BF16),
            pltpu.VMEM((q_cols, model), BF16),
            pltpu.VMEM((TP * CHUNKS, 1, piece), F32),
            pltpu.VMEM((TP, 1, feat), F32),
            pltpu.VMEM((1, rows), F32),
            pltpu.VMEM((rows, 2 * kv_cols), F32),
            pltpu.VMEM((rows, q_cols), F32),
            pltpu.VMEM((rows, hd), F32),
            pltpu.VMEM((rows, hd), F32),
            pltpu.VMEM((CTX, 2, rows, kv_cols), BF16),
            pltpu.VMEM(state, BF16),
            pltpu.VMEM((kv_heads, 2 * rows, 1), F32),
            pltpu.VMEM((kv_heads, 2 * rows, 1), F32),
            pltpu.VMEM(state, F32),
            pltpu.VMEM((rows, q_cols), BF16),
            pltpu.VMEM((TP, feat, rows), BF16),
            pltpu.VMEM((TP, feat, rows), BF16),
            pltpu.VMEM((TP, feat, rows), BF16),
            pltpu.VMEM((feat, rows), F32),
            pltpu.VMEM((8, rows), F32),
            pltpu.VMEM((TP, 8, rows), F32),
            dma((TP, CHUNKS, 3)),
            dma,
            dma((TP, CHUNKS)),
            dma((TP, CHUNKS)),
            dma((TP, CHUNKS)),
            dma((3,)),
            dma((3,)),
            dma((TP, CHUNKS)),
            dma((TP, CHUNKS)),
            dma((TP, CHUNKS)),
            dma((TP, CHUNKS)),
            dma((TP,)),
            dma((TP,)),
        ],
        compiler_params=pltpu.CompilerParams(
            collective_id=0, has_side_effects=True, vmem_limit_bytes=60 * 1024 * 1024
        ),
    )(
        tokens.T,
        positions.reshape(1, rows),
        first_key.reshape(1, rows),
        input_gain,
        query_gain.reshape(1, hd),
        key_gain.reshape(1, hd),
        post_gain,
        query_weight,
        kv_weight,
        out_weight,
    ).T


def solution(mesh):
    fused = mesh.shape["tp"] == TP and mesh.shape["ctx"] == CTX
    return jax.shard_map(
        per_device_fused if fused else per_device,
        mesh=mesh,
        in_specs=(
            P(("group", "ctx"), "tp"),
            P(("group", "ctx")),
            P(("group", "ctx")),
            P(),
            P(None, "tp"),
            P(None, None, "tp"),
            P(),
            P(),
            P("tp", None),
            P(),
        ),
        out_specs=P(("group", "ctx"), "tp"),
        check_vma=False,
    )
```
